256 devices in a mesh: panel: 8 (over z), tx: 8 (over y, x_lo), ty: 4 (over x_hi, core).
Axes of the slice: x: 4 (x_hi: 2, x_lo: 2; x = x_hi * 2 + x_lo), y: 4, z: 8, core: 2. Of those that a mesh axis runs over, the one named last changes fastest.
Arguments:
- cotangent: float32 [70, 512, 512], P(None, ('panel', 'tx'), 'ty'), may hold values from -30 to 30
- courant: float32 [70, 512, 512], P(None, ('panel', 'tx'), 'ty'), may hold values from 0.1 to 0.9
- faces_first: float32 [70, 512, 512], P(None, ('panel', 'tx'), 'ty'), may hold values from 0.1 to 1
- faces_second: float32 [70, 512, 512], P(None, ('panel', 'tx'), 'ty'), may hold values from 0.1 to 1
- faces_vertical: float32 [69, 512, 512], P(None, ('panel', 'tx'), 'ty'), may hold values from 0.5 to 8
- damping: float32 [70, 512, 512], P(None, ('panel', 'tx'), 'ty'), may hold values from 0.0005 to 0.005
- blocks_fine: float32 [7, 10, 10, 512, 512], P(None, None, None, ('panel', 'tx'), 'ty'), may hold values from 0 to 4
- blocks_half: float32 [7, 10, 10, 256, 256], P(None, None, None, ('panel', 'tx'), 'ty'), may hold values from 0 to 4
- blocks_quarter: float32 [7, 10, 10, 128, 128], P(None, None, None, ('panel', 'tx'), 'ty'), may hold values from 0 to 4
- blocks_eighth: float32 [7, 10, 10, 64, 64], P(None, None, None, ('panel', 'tx'), 'ty'), may hold values from 0 to 4
Outputs:
- solution: float32 [70, 512, 512], P(None, ('panel', 'tx'), 'ty')
- residual: float32 [70, 512, 512], P(None, ('panel', 'tx'), 'ty')
The draws below stay inside these ranges and needn't reach their ends.
All inputs are finite; a program needn't handle non-finite values.
Results may differ from the reference program's by a relative error of at most 0.0003.
Values sent between devices are 32-bit elements; how exact they have to be, the bound alone decides.
No kernel may reach another device: no remote copies, remote signals or barrier semaphores. Data moves between devices by JAX's collectives and lax.ppermute only.
A program may use at most 128 MiB of HBM per device.

```python
import jax
import jax.numpy as jnp
from jax import lax

LEV = 70
BLK = 10
GRIDS = 4
ITERS = 3
NA = 512
NB = 512


def loguniform(key, shape, low, high):
    return jnp.exp(jax.random.uniform(key, shape, jnp.float32, jnp.log(low), jnp.log(high)))


def coefficients(key):
    shape = (LEV, NA, NB)
    first = loguniform(jax.random.fold_in(key, 7001), shape, 0.1, 1.0)
    second = loguniform(jax.random.fold_in(key, 7002), shape, 0.1, 1.0)
    vertical = loguniform(jax.random.fold_in(key, 7003), (LEV - 1, NA, NB), 0.5, 8.0)
    damping = loguniform(jax.random.fold_in(key, 7004), shape, 0.0005, 0.005)
    return (first, second, vertical, damping)


def pick_drawn(values, first, second):
    levels, rows, cols = values.shape
    return values.reshape(levels, rows // 2, 2, cols // 2, 2)[:, :, first, :, second]


def restrict_drawn(values):
    levels, rows, cols = values.shape
    return values.reshape(levels, rows // 2, 2, cols // 2, 2).sum(axis=(2, 4))


def coarsen_drawn(weights):
    upper_first, lower_first, upper_second, lower_second, vertical, damping = weights
    return (pick_drawn(upper_first, 1, 0) + pick_drawn(upper_first, 1, 1), pick_drawn(lower_first, 0, 0) + pick_drawn(lower_first, 0, 1), pick_drawn(upper_second, 0, 1) + pick_drawn(upper_second, 1, 1), pick_drawn(lower_second, 0, 0) + pick_drawn(lower_second, 1, 0), restrict_drawn(vertical), restrict_drawn(damping))


def ladder_of(key):
    first, second, vertical, damping = coefficients(key)
    lower_first = jnp.roll(first, 1, axis=1)
    edge = jnp.zeros_like(second[:, :, :1])
    lower_second = jnp.concatenate([edge, second[:, :, :-1]], axis=2)
    ladder = [(first, lower_first, second, lower_second, vertical, damping)]
    for level in range(GRIDS - 1):
        ladder.append(coarsen_drawn(ladder[-1]))
    return ladder


def invert_blocks(weights):
    upper_first, lower_first, upper_second, lower_second, vertical, damping = weights
    levels, rows, cols = damping.shape
    bottom = jnp.zeros_like(vertical[:1])
    column = jnp.concatenate([vertical, bottom], axis=0)
    centre = damping + upper_first + lower_first + upper_second + lower_second
    centre = centre + column + jnp.concatenate([bottom, vertical], axis=0)
    count = levels // BLK
    centre = jnp.moveaxis(centre.reshape(count, BLK, rows, cols), 1, -1)
    couple = jnp.moveaxis(column.reshape(count, BLK, rows, cols), 1, -1)
    identity = jnp.eye(BLK, dtype=jnp.float32)
    above = jnp.eye(BLK, k=1, dtype=jnp.float32)
    below = jnp.eye(BLK, k=-1, dtype=jnp.float32)
    matrix = centre[..., :, None] * identity - couple[..., :, None] * above - couple[..., None, :] * below
    inverse = jnp.linalg.inv(matrix)
    return jnp.transpose(inverse, (0, 3, 4, 1, 2)).astype(jnp.float32)


def draw_cotangent(key, part):
    ramp = 3.0 ** (jnp.arange(NA, dtype=jnp.float32) / NA)
    spread = loguniform(jax.random.fold_in(key, 9002), (NA, NB), 1.0, 10.0)
    scale = ramp[:, None] * spread / 4.0
    values = jnp.clip(jax.random.normal(jax.random.fold_in(key, 9001), (LEV, NA, NB), jnp.float32), -4.0, 4.0)
    return (values * scale[None]).astype(jnp.float32)


def draw_faces_first(key, part):
    return coefficients(key)[0]


def draw_faces_second(key, part):
    return coefficients(key)[1]


def draw_faces_vertical(key, part):
    return coefficients(key)[2]


def draw_damping(key, part):
    return coefficients(key)[3]


def draw_blocks_fine(key, part):
    return invert_blocks(ladder_of(key)[0])


def draw_blocks_half(key, part):
    return invert_blocks(ladder_of(key)[1])


def draw_blocks_quarter(key, part):
    return invert_blocks(ladder_of(key)[2])


def draw_blocks_eighth(key, part):
    return invert_blocks(ladder_of(key)[3])


def block_scale(rng, extent, shards, smallest, largest):
    gain, own = 1.0, jax.random.fold_in(rng, 6)
    for axis_at, blocks in shards:
        heights = jnp.exp(jax.random.uniform(jax.random.fold_in(own, axis_at), (blocks,), jnp.float32, smallest / len(shards), largest / len(shards)))
        gain = gain * jnp.repeat(heights, extent[axis_at] // blocks).reshape([-1 if axis == axis_at else 1 for axis in range(len(extent))])
    return gain


def setup_inputs(seed: int = 0) -> dict:
    keys = jax.random.split(jax.random.key(seed), 11)
    return {
        "cotangent": draw_cotangent(jax.random.fold_in(keys[10], 71), 0),
        "courant": jnp.clip(0.1 + 0.79999997 * jax.random.uniform(keys[1], (LEV, NA, NB), jnp.float32) ** block_scale(keys[1], (LEV, NA, NB), ((1, 64), (2, 4)), -0.2, 0.2), 0.1, 0.9),
        "faces_first": draw_faces_first(jax.random.fold_in(keys[10], 71), 0),
        "faces_second": draw_faces_second(jax.random.fold_in(keys[10], 71), 0),
        "faces_vertical": draw_faces_vertical(jax.random.fold_in(keys[10], 71), 0),
        "damping": draw_damping(jax.random.fold_in(keys[10], 71), 0),
        "blocks_fine": draw_blocks_fine(jax.random.fold_in(keys[10], 71), 0),
        "blocks_half": draw_blocks_half(jax.random.fold_in(keys[10], 71), 0),
        "blocks_quarter": draw_blocks_quarter(jax.random.fold_in(keys[10], 71), 0),
        "blocks_eighth": draw_blocks_eighth(jax.random.fold_in(keys[10], 71), 0),
    }


OMEGA = 0.8

def neighbours(field):
    upper_first = jnp.roll(field, -1, axis=1)
    lower_first = jnp.roll(field, 1, axis=1)
    edge = jnp.zeros_like(field[:, :, :1])
    upper_second = jnp.concatenate([field[:, :, 1:], edge], axis=2)
    lower_second = jnp.concatenate([edge, field[:, :, :-1]], axis=2)
    return (upper_first, lower_first, upper_second, lower_second)

def operate(field, weights):
    upper_first, lower_first, upper_second, lower_second, vertical, damping = weights
    beyond_up, beyond_low, across_up, across_low = neighbours(field)
    total = damping * field + upper_first * (field - beyond_up) + lower_first * (field - beyond_low)
    total = total + upper_second * (field - across_up) + lower_second * (field - across_low)
    flux = vertical * (field[1:] - field[:-1])
    bottom = jnp.zeros_like(field[:1])
    return total - jnp.concatenate([flux, bottom], axis=0) + jnp.concatenate([bottom, flux], axis=0)

def pick(values, first, second):
    levels, rows, cols = values.shape
    return values.reshape(levels, rows // 2, 2, cols // 2, 2)[:, :, first, :, second]

def restrict(values):
    levels, rows, cols = values.shape
    return values.reshape(levels, rows // 2, 2, cols // 2, 2).sum(axis=(2, 4))

def prolong(values):
    return jnp.repeat(jnp.repeat(values, 2, axis=1), 2, axis=2)

def coarsen(weights):
    upper_first, lower_first, upper_second, lower_second, vertical, damping = weights
    return (pick(upper_first, 1, 0) + pick(upper_first, 1, 1), pick(lower_first, 0, 0) + pick(lower_first, 0, 1), pick(upper_second, 0, 1) + pick(upper_second, 1, 1), pick(lower_second, 0, 0) + pick(lower_second, 1, 0), restrict(vertical), restrict(damping))

def block_solve(inverse, field):
    count, width = (inverse.shape[0], inverse.shape[1])
    levels, rows, cols = field.shape
    stacked = field.reshape(count, width, rows, cols)
    product = jnp.einsum('kijab,kjab->kiab', inverse, stacked, precision=lax.Precision.HIGHEST)
    return product.reshape(levels, rows, cols)

def cycle(level, rhs, ladder, blocks):
    weights = ladder[level]
    inverse = blocks[level]
    first = OMEGA * block_solve(inverse, rhs)
    if level == len(blocks) - 1:
        return first + OMEGA * block_solve(inverse, rhs - operate(first, weights))
    remainder = rhs - operate(first, weights)
    coarse = cycle(level + 1, restrict(remainder), ladder, blocks)
    second = first + prolong(coarse)
    return second + OMEGA * block_solve(inverse, rhs - operate(second, weights))

def reference(cotangent, courant, faces_first, faces_second, faces_vertical, damping, blocks_fine, blocks_half, blocks_quarter, blocks_eighth):
    bottom = jnp.zeros_like(cotangent[:1])
    forcing = (1.0 - courant) * cotangent + jnp.concatenate([courant[1:] * cotangent[1:], bottom], axis=0)
    lower_first = jnp.roll(faces_first, 1, axis=1)
    edge = jnp.zeros_like(faces_second[:, :, :1])
    lower_second = jnp.concatenate([edge, faces_second[:, :, :-1]], axis=2)
    weights = (faces_first, lower_first, faces_second, lower_second, faces_vertical, damping)
    ladder = [weights]
    for level in range(GRIDS - 1):
        ladder.append(coarsen(ladder[-1]))
    blocks = (blocks_fine, blocks_half, blocks_quarter, blocks_eighth)
    solution = jnp.zeros_like(forcing)
    residual = forcing
    precond = cycle(0, residual, ladder, blocks)
    direction = precond
    gamma = jnp.sum(residual * precond)
    for step in range(ITERS):
        image = operate(direction, weights)
        alpha = gamma / jnp.sum(direction * image)
        solution = solution + alpha * direction
        residual = residual - alpha * image
        if step + 1 < ITERS:
            precond = cycle(0, residual, ladder, blocks)
            fresh = jnp.sum(residual * precond)
            direction = precond + fresh / gamma * direction
            gamma = fresh
    return (solution, residual)
```

```python
import functools

import jax
import jax.numpy as jnp
from jax import lax
from jax.experimental import pallas as pl
from jax.experimental.pallas import tpu as pltpu
from jax.sharding import PartitionSpec as P

ROWS_AX = ("panel", "tx")
COLS_AX = "ty"
ALL = ("panel", "tx", "ty")

LEV = 70
BLK = 10
NBLK = 7
SUB = 8
OWN = 8
LANES = 128
WIDE = 256
EDGE = 24
PACK = 5
DEEP = 3
OMEGA = 0.8
KEEP = 1.0 - OMEGA
THETA = 1.0

F32 = jnp.float32
VM = pl.BlockSpec(memory_space=pltpu.VMEM)
SM = pl.BlockSpec(memory_space=pltpu.SMEM)
LEVELS = tuple(range(BLK))


def params():
    return pltpu.CompilerParams(vmem_limit_bytes=12 << 20)


def shape(*dims):
    return jax.ShapeDtypeStruct(dims, F32)


def call(body, outs, ins, scratch=()):
    specs = [SM if x.dtype == jnp.int32 else VM for x in ins]
    return pl.pallas_call(
        body,
        out_shape=list(outs),
        in_specs=specs,
        out_specs=[VM] * len(outs),
        scratch_shapes=list(scratch),
        compiler_params=params(),
    )(*ins)


def lane(width):
    return lax.broadcasted_iota(jnp.int32, (SUB, width), 1)


def turn(x, by):
    return pltpu.roll(x, by % x.shape[1], 1)


def down(x):
    return pltpu.roll(x, 1, 0)


def up(x):
    return pltpu.roll(x, SUB - 1, 0)


def pair_sum(x, step):
    bit = (lane(x.shape[1]) & step) == 0
    return x + jnp.where(bit, turn(x, -step), turn(x, step))


def odd_of_pair(x, step):
    bit = (lane(x.shape[1]) & step) == 0
    return jnp.where(bit, turn(x, -step), x)


def smooth(rhs, m, inv, at):
    y = [rhs[0]]
    for a in LEVELS[1:]:
        y.append(rhs[a] + m[at, a] * y[a - 1])
    x = [None] * BLK
    x[BLK - 1] = y[BLK - 1] * inv[at, BLK - 1]
    for a in LEVELS[-2::-1]:
        x[a] = y[a] * inv[at, a] + m[at, a + 1] * x[a + 1]
    return x


def coupled(x, xo, uf, us, m, co, row, step):
    out = []
    for a in LEVELS:
        here = x[row + xo, a]
        flow = us[row + co, a] * turn(here, -step) + turn(us[row + co, a] * here, step)
        flow = flow + uf[row + co, a] * x[row + xo + 1, a]
        flow = flow + uf[row + co - 1, a] * x[row + xo - 1, a]
        out.append(flow)
    edge = m[row + co, 0]
    out[0] = out[0] + down(edge * x[row + xo, BLK - 1])
    out[BLK - 1] = out[BLK - 1] + edge * up(x[row + xo, 0])
    return out


def factor(uf, us, v, dl, m, inv, o, row, step, inside):
    m[row + o, 0] = v[row + o, BLK - 1]
    beyond = down(v[row + o, BLK - 1])
    last = None
    for a in LEVELS:
        d = dl[row + o, a] + uf[row + o, a] + us[row + o, a]
        d = d + turn(us[row + o, a], step) + v[row + o, a] + beyond
        if a:
            link = beyond * last
            m[row + o, a] = link
            d = d - beyond * link
        last = 1.0 / d
        inv[row + o, a] = jnp.where(inside, OMEGA * last, 0.0)
        beyond = v[row + o, a]


def rows(low, high, body, by=2):
    trips, rest = divmod(high - low, by)

    def trip(i, carry):
        for k in range(by):
            body(low + i * by + k)
        return carry

    lax.fori_loop(0, trips, trip, 0)
    for k in range(rest):
        body(low + trips * by + k)


def packed(values, of_last):
    out = jnp.zeros((SUB, LANES), F32)
    spot = lane(LANES) // EDGE
    for f, value in enumerate(values):
        shift = EDGE * f - (LANES - EDGE) if of_last else EDGE * f
        out = jnp.where(spot == f, turn(value, shift), out)
    return out


def beyond_tile(right, left, f, has_right, has_left):
    spot = lane(LANES)
    r = jnp.where(spot < has_right, turn(right, -EDGE * f), 0.0)
    return jnp.where(spot >= has_left, turn(left, LANES - EDGE - EDGE * f), r)


def limits(pos, count):
    has_right = jnp.where(pos == count - 1, 0, EDGE)
    has_left = jnp.where(pos == 0, LANES, LANES - EDGE)
    return has_right, has_left


def squeeze_row(dst, at, values):
    quarter = lane(LANES) & 3
    for i in range(BLK // 2):
        first, second = values[2 * i], values[2 * i + 1]
        out = jnp.where(quarter == 0, first[:, :LANES], first[:, LANES:])
        other = jnp.where(quarter == 2, second[:, :LANES], second[:, LANES:])
        dst[at * (BLK // 2) + i] = jnp.where(quarter < 2, out, other)


def spread_many(src, at):
    n = BLK // 2
    lanes_in = lax.broadcasted_iota(jnp.int32, (LANES, 4 * LANES), 0)
    lanes_out = lax.broadcasted_iota(jnp.int32, (LANES, 4 * LANES), 1)
    pick = ((lanes_out & (LANES - 4)) + lanes_out // LANES == lanes_in).astype(F32)
    p = src[at * n : at * n + n].reshape(n * SUB, LANES)
    full = jnp.dot(p, pick, precision=lax.Precision.HIGHEST, preferred_element_type=F32).reshape(n, SUB, 4 * LANES)
    return [full[a // 2, :, WIDE * (a % 2) : WIDE * (a % 2 + 1)] for a in LEVELS]


def spread_row(src, at):
    bits = lane(LANES)
    out = []
    for i in range(BLK // 2):
        p = src[at * (BLK // 2) + i]
        even = (bits & 1) == 0
        fill = (jnp.where(even, p, turn(p, 1)), jnp.where(even, turn(p, -1), p))
        low = (bits & 2) == 0
        for half in (0, 1):
            tiles = []
            for t in fill:
                tiles.append(jnp.where(low, t, turn(t, 2)) if half == 0 else jnp.where(low, turn(t, -2), t))
            out.append(jnp.concatenate(tiles, axis=1))
    return out


def halve_row(dst, at, values):
    even = (lane(LANES) & 1) == 0
    for a in LEVELS:
        dst[at + a] = jnp.where(even, values[a][:, :LANES], values[a][:, LANES:])


def double_row(src, at):
    even = (lane(LANES) & 1) == 0
    out = []
    for a in LEVELS:
        p = src[at + a]
        out.append(jnp.concatenate([jnp.where(even, p, turn(p, 1)), jnp.where(even, turn(p, -1), p)], axis=1))
    return out


def put(ref, at, values):
    for a in LEVELS:
        ref[at, a] = values[a]


def row_of(ref, at):
    return [ref[at, a] for a in LEVELS]


def first_kernel(*refs):
    far_in, (own, msg_a, msg_b, to_right, to_left, start), near_in, sem = refs[:6], refs[6:12], refs[12:18], refs[18]
    copies = [pltpu.make_async_copy(far_in[i], near_in[i], sem.at[i]) for i in range(6)]
    for copy in copies:
        copy.start()
    for copy in copies:
        copy.wait()
    cot, cour, ff, fs, fv, damp = near_in
    none = jnp.zeros((SUB - NBLK, LANES), F32)

    def read(ref, level, row, count=NBLK):
        got = ref[pl.ds(level * OWN + row, count, stride=BLK * OWN), :]
        if count < NBLK:
            got = jnp.concatenate([got, jnp.zeros((NBLK - count, LANES), F32)], axis=0)
        return jnp.concatenate([got, none], axis=0)

    def per_row(row, carry):
        for a in LEVELS:
            c, t = read(cour, a, row), read(cot, a, row)
            if a < BLK - 1:
                nc, nt = read(cour, a + 1, row), read(cot, a + 1, row)
                v = read(fv, a, row)
            else:
                nc, nt = read(cour, BLK, row, NBLK - 1), read(cot, BLK, row, NBLK - 1)
                v = read(fv, a, row, NBLK - 1)
            plain = read(damp, a, row)
            dl = plain + jnp.where(row > 0, read(ff, a, jnp.maximum(row - 1, 0)), 0.0)
            values = ((1.0 - c) * t + nc * nt, read(ff, a, row), read(fs, a, row), v, dl)
            for f, value in enumerate(values):
                own[row, f * BLK + a] = value
            own[row, 5 * BLK + a] = plain
            start[row, a] = values[0]
            to_right[row, a] = packed(values, True)
            to_left[row, a] = packed(values, False)
        return carry

    lax.fori_loop(0, OWN, per_row, 0)

    def per_edge(i, carry):
        for j in range(5 * BLK):
            msg_a[i, j] = own[i + OWN - DEEP, j]
            msg_b[i, j] = own[i, j]
        return carry

    lax.fori_loop(0, DEEP, per_edge, 0)


def descend(r0, x0, r1, x1, r2, c0, c1):
    (uf0, us0, m0, i0), (uf1, us1, m1, i1) = c0, c1
    rows(-3, 11, lambda row: pre(r0, x0, m0, i0, 3, row))

    def to1(coarse):
        put(r1, coarse + 2, below(r0, x0, uf0, us0, m0, 3, 1, coarse))

    rows(-1, 5, to1, 1)
    rows(-1, 5, lambda row: pre(r1, x1, m1, i1, 2, row))
    for coarse in (0, 1):
        put(r2, coarse, below(r1, x1, uf1, us1, m1, 2, 2, coarse))


def pre(r, x, m, inv, o, row):
    put(x, row + o, smooth(row_of(r, row + o), m, inv, row + o))


def below(r, x, uf, us, m, o, step, coarse):
    total = None
    for row in (2 * coarse, 2 * coarse + 1):
        near = coupled(x, o, uf, us, m, o, row, step)
        near = [near[a] + KEEP * r[row + o, a] for a in LEVELS]
        total = near if total is None else [total[a] + near[a] for a in LEVELS]
    return [pair_sum(t, step) for t in total]


def coarse_message(r1, r2, up_msg, down_msg):
    for dst, row in ((up_msg, 2), (down_msg, 1)):
        halve_row(dst, 0, row_of(r1, row + 2))
        for k in (0, 1):
            squeeze_row(dst.at[BLK:], k, row_of(r2, k))


def fill_rows(dst, o, base, count, own, edges, pos_limits, slots):
    has_right, has_left = pos_limits

    def one(i, carry):
        for a in LEVELS:
            dst[base + i + o, a, :, :LANES] = own(i, a)
            left, right = edges(i, a)
            dst[base + i + o, a, :, LANES:] = beyond_tile(right, left, slots(a), has_right, has_left)
        return carry

    lax.fori_loop(0, count, one, 0)


def setup_kernel(count, pos, own, got_l, got_r, own_a, own_b, got_a, got_b, *refs):
    r0, x0, uf0, us0, m0, i0, r1, x1, uf1, us1, m1, i1, r2, uf2, us2, m2, i2, up_msg, down_msg = refs[:19]
    up_co, down_co, far_co = refs[19:22]
    v0, d0, v1, d1, v2, d2, uf3, us3, v3, d3, m3, i3 = refs[22:]
    lim = limits(pos[0], count)
    for f, dst in enumerate((r0, uf0, us0, v0, d0)):
        for base, num, src, edge in (
            (0, OWN, own, (got_l, got_r)),
            (-DEEP, DEEP, own_a, got_a),
            (OWN, DEEP, own_b, got_b),
        ):
            if isinstance(edge, tuple):
                edges = lambda i, a, e=edge: (e[0][i, a], e[1][i, a])
            else:
                edges = lambda i, a, e=edge: (e[i, a], e[i, a + BLK])
            fill_rows(dst, 3, base, num, lambda i, a, s=src, f=f: s[i, f * BLK + a], edges, lim, lambda a, f=f: f)
    spot = lane(WIDE)
    sub = lax.broadcasted_iota(jnp.int32, (SUB, WIDE), 0)
    inside = (sub < NBLK) & ((spot < LANES + lim[0]) | (spot >= LANES + lim[1]))
    for row in (0, OWN):
        for a in LEVELS:
            d0[row + 3, a] = d0[row + 3, a] + uf0[row + 2, a]

    def ready(row):
        for a in LEVELS:
            d0[row + 3, a] = jnp.where(inside, d0[row + 3, a], 1.0)
        factor(uf0, us0, v0, d0, m0, i0, 3, row, 1, inside)

    rows(-3, 11, ready)

    def coarsen(low, high, fine, fo, coarse, co, step, m, inv):
        uf, us, v, d = fine
        cuf, cus, cv, cd = coarse
        put(cuf, low - 1 + co, [pair_sum(t, step) for t in row_of(uf, 2 * low - 1 + fo)])

        def one(row):
            p, q = 2 * row + fo, 2 * row + 1 + fo
            for a in LEVELS:
                cuf[row + co, a] = pair_sum(uf[q, a], step)
                cus[row + co, a] = odd_of_pair(us[p, a] + us[q, a], step)
                cv[row + co, a] = pair_sum(v[p, a] + v[q, a], step)
                cd[row + co, a] = pair_sum(d[p, a] + (d[q, a] - uf[p, a]), step)
            factor(cuf, cus, cv, cd, m, inv, co, row, 2 * step, inside)

        rows(low, high, one, 1)

    coarsen(-1, 5, (uf0, us0, v0, d0), 3, (uf1, us1, v1, d1), 2, 1, m1, i1)
    coarsen(0, 2, (uf1, us1, v1, d1), 2, (uf2, us2, v2, d2), 1, 2, m2, i2)
    coarsen(0, 1, (uf2, us2, v2, d2), 1, (uf3, us3, v3, d3), 1, 4, m3, i3)
    for dst, row in ((up_co, 2), (down_co, 1)):
        halve_row(dst, 0, row_of(m1, row + 2))
        halve_row(dst, BLK, row_of(i1, row + 2))
        at = dst.at[2 * BLK :]
        for f, ref in enumerate((m2, i2, uf2, us2)):
            for k in (0, 1):
                squeeze_row(at, 2 * f + k, row_of(ref, k + 1))
        for f, ref in enumerate((m3, i3, uf3, us3)):
            squeeze_row(at, 8 + f, row_of(ref, 1))
    for f, ref in enumerate((m3, i3, uf3, us3)):
        squeeze_row(far_co, f, row_of(ref, 1))
    descend(r0, x0, r1, x1, r2, (uf0, us0, m0, i0), (uf1, us1, m1, i1))
    coarse_message(r1, r2, up_msg, down_msg)


def coarse_kernel(uf2, us2, m2, i2, co_a, co_b, far_co, far_a, far_b, *outs):
    edge1, outs2, outs3 = outs[:2], outs[2:6], outs[6:10]
    for f in range(2):
        put(edge1[f], 0, double_row(co_a, f * BLK))
        put(edge1[f], 1, double_row(co_b, f * BLK))
    at_a, at_b = co_a.at[2 * BLK :], co_b.at[2 * BLK :]
    for f, (dst, own) in enumerate(zip(outs2, (m2, i2, uf2, us2))):
        for k in (0, 1):
            put(dst, k, spread_many(at_a, 2 * f + k))
            put(dst, k + 2, row_of(own, k + 1))
            put(dst, k + 4, spread_many(at_b, 2 * f + k))
    for f, dst in enumerate(outs3):
        put(dst, 0, spread_many(far_a, f))
        put(dst, 1, spread_many(at_a, 8 + f))
        put(dst, 2, spread_many(far_co, f))
        put(dst, 3, spread_many(at_b, 8 + f))
        put(dst, 4, spread_many(far_b, f))


def again_kernel(count, pos, own, got_l, got_r, all_a, all_b, *refs):
    c0, c1 = refs[:4], refs[4:8]
    r0, x0, r1, x1, r2, up_msg, down_msg = refs[8:]
    lim = limits(pos[0], count)
    slots = lambda a: a % PACK
    fill_rows(
        r0, 3, 0, OWN, lambda i, a: own[i, a],
        lambda i, a: (got_l[i, a // PACK], got_r[i, a // PACK]), lim, slots,
    )
    for base, src in ((-DEEP, all_a), (OWN, all_b)):
        fill_rows(
            r0, 3, base, DEEP, lambda i, a, s=src: s[i, a],
            lambda i, a, s=src: (s[i, BLK + a // PACK], s[i, BLK + 2 + a // PACK]), lim, slots,
        )
    descend(r0, x0, r1, x1, r2, c0, c1)
    coarse_message(r1, r2, up_msg, down_msg)


def middle_kernel(r2_own, got_a, got_b, m2, i2, uf2, us2, r2, x2, r3, msg):
    for k in (0, 1):
        put(r2, k, spread_row(got_a.at[BLK:], k))
        put(r2, k + 2, row_of(r2_own, k))
        put(r2, k + 4, spread_row(got_b.at[BLK:], k))
    rows(-2, 4, lambda row: pre(r2, x2, m2, i2, 2, row))
    got = below(r2, x2, uf2, us2, m2, 2, 4, 0)
    put(r3, 0, got)
    squeeze_row(msg, 0, got)


def ascend_kernel(number, *refs):
    refs = list(refs)
    take = lambda n: [refs.pop(0) for _ in range(n)]
    r_own, own, got_a, got_b, r3_own, near_a, near_b, far_a, far_b = take(9)
    r0, x0_in, r1_in, x1_in, r2, x2_in = take(6)
    uf0, us0, m0, i0 = take(4)
    uf1, us1, m1, i1, m1_edge, i1_edge = take(6)
    m2, i2, uf2, us2, m3, i3, uf3, us3 = take(8)
    past = []
    if number == 2:
        past = take(5)
        first_r = take(1)[0]
    z_own, w_own = take(2)
    if number < 2:
        r_next, to_right, to_left = take(3)
    else:
        gram = take(1)[0]
    x2, r3, x3, e3, e2, e1, z0, x1, x0, r_edge = take(10)

    put(r3, 0, spread_row(far_a, 0))
    put(r3, 1, spread_row(near_a, 0))
    put(r3, 2, row_of(r3_own, 0))
    put(r3, 3, spread_row(near_b, 0))
    put(r3, 4, spread_row(far_b, 0))
    rows(0, 5, lambda at: pre(r3, x3, m3, i3, 0, at))

    def post(r, x, uf, us, m, inv, o, step, row):
        near_x = coupled(x, 2, uf, us, m, o, row, step)
        got = smooth([near_x[a] + r[row + o, a] for a in LEVELS], m, inv, row + o)
        return [got[a] + KEEP * x[row + 2, a] for a in LEVELS]

    for row in (-1, 0, 1):
        put(e3, row + 1, post(r3, x3, uf3, us3, m3, i3, 2, 8, row))
    put(r_edge, 0, double_row(got_a, 0))
    put(r_edge, 1, double_row(got_b, 0))

    def add(dst, do, x, o, e, coarse):
        for row in (2 * coarse, 2 * coarse + 1):
            for a in LEVELS:
                dst[row + do, a] = x[row + o, a] + e[coarse + 1, a]

    rows(-1, 2, lambda c: add(x2, 2, x2_in, 2, e3, c), 1)
    rows(-1, 3, lambda row: put(e2, row + 1, post(r2, x2, uf2, us2, m2, i2, 2, 4, row)))
    rows(0, 2, lambda c: add(x1, 2, x1_in, 2, e2, c), 1)
    for at, row, coarse in ((0, -2, -1), (1, 5, 2)):
        outer = smooth(row_of(r_edge, at), m1_edge, i1_edge, at)
        inner = row_of(x1_in, (-1 if at == 0 else 4) + 2)
        for a in LEVELS:
            x1[row + 2, a] = outer[a] + e2[coarse + 1, a]
            x1[(-1 if at == 0 else 4) + 2, a] = inner[a] + e2[coarse + 1, a]
    rows(-1, 5, lambda row: put(e1, row + 1, post(r1_in, x1, uf1, us1, m1, i1, 2, 2, row)))
    rows(-1, 5, lambda c: add(x0, 2, x0_in, 3, e1, c), 1)
    rows(-1, 9, lambda row: put(z0, row + 1, post(r0, x0, uf0, us0, m0, i0, 3, 1, row)))

    def image(row):
        flux = None
        last = z0[row + 1, BLK - 1][:, :LANES]
        first_z = z0[row + 1, 0][:, :LANES]
        over = own[row, 3 * BLK + BLK - 1] * (up(first_z) - last)
        below = down(over)
        for a in LEVELS:
            wide = z0[row + 1, a]
            here = wide[:, :LANES]
            side = us0[row + 3, a] * (wide - turn(wide, -1))
            total = own[row, 5 * BLK + a] * here + (side - turn(side, 1))[:, :LANES]
            total = total + uf0[row + 3, a][:, :LANES] * (here - z0[row + 2, a][:, :LANES])
            total = total + uf0[row + 2, a][:, :LANES] * (here - z0[row, a][:, :LANES])
            if a < BLK - 1:
                flux = own[row, 3 * BLK + a] * (z0[row + 1, a + 1][:, :LANES] - here)
            else:
                flux = over
            total = total - flux + below
            below = flux
            w_own[row, a] = total
            z_own[row, a] = here
            if number < 2:
                r_next[row, a] = r_own[row, a] - THETA * total
        if number < 2:
            for g in range(BLK // PACK):
                values = [r_next[row, g * PACK + f] for f in range(PACK)]
                to_right[row, g] = packed(values, True)
                to_left[row, g] = packed(values, False)

    rows(0, OWN, image, 1)

    if number == 2:
        g_r0, g_z0, g_w0, g_z1, g_w1 = past

        def dots(row, acc):
            acc = list(acc)
            for a in LEVELS:
                z = (g_z0[row, a], g_z1[row, a], z_own[row, a])
                w = (g_w0[row, a], g_w1[row, a], w_own[row, a])
                r = (g_r0[row, a], first_r[row, a], r_own[row, a])
                terms = [r[i] * z[j] for i in range(3) for j in range(i + 1)]
                terms += [w[i] * z[j] for i in range(3) for j in range(3)]
                acc = [s + t for s, t in zip(acc, terms)]
            return tuple(acc)

        acc = lax.fori_loop(0, OWN, dots, tuple(jnp.zeros((SUB, LANES), F32) for _ in range(15)))
        gram[...] = jnp.zeros_like(gram)
        for i in range(15):
            gram[i : i + 1, :] = jnp.sum(acc[i], axis=0, keepdims=True)


def last_kernel(gram, r2, z0, z1, z2, w0, w1, w2, sol, res):
    get = lambda i: jnp.broadcast_to(jnp.sum(gram[i : i + 1, :], axis=1, keepdims=True), (SUB, LANES))
    q, at = {}, 0
    for i in range(3):
        for j in range(i + 1):
            q["r", i, j] = get(at)
            at += 1
    for i in range(3):
        for j in range(3):
            q["w", i, j] = get(at)
            at += 1
    zero = jnp.zeros((SUB, LANES), F32)

    def product(base, c, z):
        total = zero
        for j in range(3):
            if z[j] is None:
                continue
            term = q["r", base, j] if base is not None else zero
            for i in range(3):
                if c[i] is not None:
                    term = term + c[i] * q["w", i, j]
            total = total + z[j] * term
        return total

    one = zero + 1.0
    c = [None] * 3
    p = [one, None, None]
    gamma = q["r", 0, 0]
    x = [zero] * 3
    plus = lambda s, t: t if s is None else s + t
    for step in range(3):
        alpha = gamma / product(None, p, p)
        for j in range(step + 1):
            x[j] = x[j] + alpha * p[j]
            c[j] = plus(c[j], -(alpha * p[j]))
        if step == 2:
            break
        c[step] = c[step] + THETA
        z = [None] * 3
        z[step + 1] = one
        for i in range(step + 1):
            part = c[i] * (1.0 / THETA)
            z[i] = plus(z[i], part)
            z[i + 1] = plus(z[i + 1], -part)
        fresh = product(step + 1, c, z)
        beta = fresh / gamma
        p = [plus(z[j], beta * p[j]) if p[j] is not None else z[j] for j in range(3)]
        gamma = fresh

    def per_row(row, carry):
        for a in LEVELS:
            s = x[0] * z0[row, a] + x[1] * z1[row, a] + x[2] * z2[row, a]
            t = r2[row, a] + c[0] * w0[row, a] + c[1] * w1[row, a] + c[2] * w2[row, a]
            sol[pl.ds(a * OWN + row, NBLK, stride=BLK * OWN), :] = s[:NBLK]
            res[pl.ds(a * OWN + row, NBLK, stride=BLK * OWN), :] = t[:NBLK]
        return carry

    lax.fori_loop(0, OWN, per_row, 0)


def per_device(cotangent, courant, faces_first, faces_second, faces_vertical, damping, *blocks):
    n_rows = lax.axis_size(ROWS_AX)
    n_cols = lax.axis_size(COLS_AX)
    pos = lax.axis_index(COLS_AX).reshape(1).astype(jnp.int32)

    def send(x, dr, dc):
        route = [
            (r * n_cols + c, ((r + dr) % n_rows) * n_cols + (c + dc) % n_cols)
            for r in range(n_rows)
            for c in range(n_cols)
        ]
        return lax.ppermute(x, ALL, route)

    def total_over(x, axis):
        size, done = lax.axis_size(axis), 1
        while done < size:
            count = min(4, size // done)
            route = lambda by: [(i, (i + by) % size) for i in range(size)]
            x = functools.reduce(jnp.add, [lax.ppermute(x, axis, route(k * done)) for k in range(1, count)], x)
            done *= count
        return x

    flat = lambda x: x.reshape(x.shape[0] * OWN, LANES)
    wide = lambda n: shape(n, BLK, SUB, WIDE)
    tile = lambda *n: shape(*n, SUB, LANES)
    vwide = lambda n: pltpu.VMEM((n, BLK, SUB, WIDE), F32)

    own, msg_a, msg_b, to_right, to_left, start = pl.pallas_call(
        first_kernel,
        out_shape=[
            tile(OWN, 6 * BLK), tile(DEEP, 5 * BLK), tile(DEEP, 5 * BLK),
            tile(OWN, BLK), tile(OWN, BLK), tile(OWN, BLK),
        ],
        in_specs=[pl.BlockSpec(memory_space=pltpu.HBM)] * 6,
        out_specs=[VM] * 6,
        scratch_shapes=[pltpu.VMEM(((LEV - (i == 4)) * OWN, LANES), F32) for i in range(6)]
        + [pltpu.SemaphoreType.DMA((6,))],
        compiler_params=params(),
    )(*[pltpu.with_memory_space_constraint(flat(x), pltpu.HBM) for x in (cotangent, courant, faces_first, faces_second, faces_vertical, damping)])
    own_a, own_b = send(msg_a, 1, 0), send(msg_b, -1, 0)
    got_l, got_r = send(to_right, 0, 1), send(to_left, 0, -1)
    got_a = send(jnp.concatenate([got_l[-DEEP:], got_r[-DEEP:]], axis=1), 1, 0)
    got_b = send(jnp.concatenate([got_l[:DEEP], got_r[:DEEP]], axis=1), -1, 0)

    outs = call(
        functools.partial(setup_kernel, n_cols),
        [wide(14)] * 6 + [wide(8)] * 6 + [wide(2)] + [wide(3)] * 4 + [tile(20)] * 2 + [tile(80)] * 2 + [tile(20)],
        [pos, own, got_l, got_r, own_a, own_b, got_a, got_b],
        [vwide(n) for n in (14, 14, 8, 8, 3, 3, 3, 3, 3, 3, 3, 3)],
    )
    r0, x0, uf0, us0, m0, i0, r1, x1, uf1, us1, m1, i1, r2, uf2, us2, m2, i2, up_msg, down_msg = outs[:19]
    up_co, down_co, far_co = outs[19:]
    c0, c1 = (uf0, us0, m0, i0), (uf1, us1, m1, i1)
    co_a, co_b = send(up_co, 1, 0), send(down_co, -1, 0)
    far_a, far_b = send(far_co, 2, 0), send(far_co, -2, 0)
    residuals, zs, ws = [start], [], []
    upward = [vwide(n) for n in (6, 5, 5, 3, 4, 6, 10, 8, 12, 2)]
    for number in range(3):
        if number:
            got_l, got_r = send(to_right, 0, 1), send(to_left, 0, -1)
            whole = jnp.concatenate([residuals[-1], got_l, got_r], axis=1)
            all_a, all_b = send(whole[OWN - DEEP :], 1, 0), send(whole[:DEEP], -1, 0)
            r0, x0, r1, x1, r2, up_msg, down_msg = call(
                functools.partial(again_kernel, n_cols),
                [wide(14)] * 2 + [wide(8)] * 2 + [wide(2)] + [tile(20)] * 2,
                [pos, residuals[-1], got_l, got_r, all_a, all_b, *c0, *c1],
            )
        msg_a, msg_b = send(up_msg, 1, 0), send(down_msg, -1, 0)
        if number == 0:
            coarse = call(
                coarse_kernel,
                [wide(2)] * 2 + [wide(6)] * 4 + [wide(5)] * 4,
                [uf2, us2, m2, i2, co_a, co_b, far_co, far_a, far_b],
            )
            edge1, c2, c3 = coarse[:2], coarse[2:6], coarse[6:]
        r2, x2, r3, msg = call(
            middle_kernel,
            [wide(6)] * 2 + [wide(1), tile(5)],
            [r2, msg_a, msg_b, *c2],
        )
        near_a, near_b = send(msg, 1, 0), send(msg, -1, 0)
        far_a, far_b = send(msg, 2, 0), send(msg, -2, 0)
        ins = [residuals[-1], own, msg_a, msg_b, r3, near_a, near_b, far_a, far_b, r0, x0, r1, x1, r2, x2]
        ins += [*c0, *c1, *edge1, *c2, *c3]
        if number == 2:
            ins += [residuals[0], zs[0], ws[0], zs[1], ws[1], residuals[1]]
        outs = [tile(OWN, BLK)] * 2
        outs += [tile(OWN, BLK), tile(OWN, 2), tile(OWN, 2)] if number < 2 else [shape(16, LANES)]
        outs = call(functools.partial(ascend_kernel, number), outs, ins, upward)
        zs.append(outs[0])
        ws.append(outs[1])
        if number < 2:
            residuals.append(outs[2])
            to_right, to_left = outs[3:]
        else:
            gram = outs[2]
    for axis in (COLS_AX, "tx", "panel"):
        gram = total_over(gram, axis)
    sol, res = call(
        last_kernel,
        [shape(LEV * OWN, LANES)] * 2,
        [gram, residuals[2], *zs, *ws],
    )
    return sol.reshape(LEV, OWN, LANES), res.reshape(LEV, OWN, LANES)


def solution(mesh):
    field = P(None, ROWS_AX, COLS_AX)
    block = P(None, None, None, ROWS_AX, COLS_AX)
    return jax.shard_map(
        per_device,
        mesh=mesh,
        in_specs=(field,) * 6 + (block,) * 4,
        out_specs=(field, field),
        check_vma=False,
    )
```

```python
import functools

import jax
import jax.numpy as jnp
from jax import lax
from jax.experimental import pallas as pl
from jax.experimental.pallas import tpu as pltpu
from jax.sharding import PartitionSpec as P

ROWS_AX = ("panel", "tx")
COLS_AX = "ty"
ALL = ("panel", "tx", "ty")

LEV = 70
BLK = 10
NBLK = 7
SUB = 8
OWN = 8
LANES = 128
WIDE = 256
EDGE = 24
PACK = 5
DEEP = 3
OMEGA = 0.8
KEEP = 1.0 - OMEGA
THETA = 1.0

F32 = jnp.float32
VM = pl.BlockSpec(memory_space=pltpu.VMEM)
SM = pl.BlockSpec(memory_space=pltpu.SMEM)
LEVELS = tuple(range(BLK))


def params():
    return pltpu.CompilerParams(vmem_limit_bytes=12 << 20)


def shape(*dims):
    return jax.ShapeDtypeStruct(dims, F32)


def call(body, outs, ins, scratch=()):
    specs = [SM if x.dtype == jnp.int32 else VM for x in ins]
    return pl.pallas_call(
        body,
        out_shape=list(outs),
        in_specs=specs,
        out_specs=[VM] * len(outs),
        scratch_shapes=list(scratch),
        compiler_params=params(),
        cost_estimate=pl.CostEstimate(flops=8_000_000, bytes_accessed=16_000_000, transcendentals=0),
    )(*ins)


def lane(width):
    return lax.broadcasted_iota(jnp.int32, (SUB, width), 1)


def turn(x, by):
    return pltpu.roll(x, by % x.shape[1], 1)


def down(x):
    return pltpu.roll(x, 1, 0)


def up(x):
    return pltpu.roll(x, SUB - 1, 0)


def pair_sum(x, step):
    bit = (lane(x.shape[1]) & step) == 0
    return x + jnp.where(bit, turn(x, -step), turn(x, step))


def odd_of_pair(x, step):
    bit = (lane(x.shape[1]) & step) == 0
    return jnp.where(bit, turn(x, -step), x)


def smooth(rhs, m, inv, at):
    y = [rhs[0]]
    for a in LEVELS[1:]:
        y.append(rhs[a] + m[at, a] * y[a - 1])
    x = [None] * BLK
    x[BLK - 1] = y[BLK - 1] * inv[at, BLK - 1]
    for a in LEVELS[-2::-1]:
        x[a] = y[a] * inv[at, a] + m[at, a + 1] * x[a + 1]
    return x


def coupled(x, xo, uf, us, m, co, row, step):
    out = []
    for a in LEVELS:
        here = x[row + xo, a]
        flow = us[row + co, a] * turn(here, -step) + turn(us[row + co, a] * here, step)
        flow = flow + uf[row + co, a] * x[row + xo + 1, a]
        flow = flow + uf[row + co - 1, a] * x[row + xo - 1, a]
        out.append(flow)
    edge = m[row + co, 0]
    out[0] = out[0] + down(edge * x[row + xo, BLK - 1])
    out[BLK - 1] = out[BLK - 1] + edge * up(x[row + xo, 0])
    return out


def factor(uf, us, v, dl, m, inv, o, row, step, inside):
    m[row + o, 0] = v[row + o, BLK - 1]
    beyond = down(v[row + o, BLK - 1])
    last = None
    for a in LEVELS:
        d = dl[row + o, a] + uf[row + o, a] + us[row + o, a]
        d = d + turn(us[row + o, a], step) + v[row + o, a] + beyond
        if a:
            link = beyond * last
            m[row + o, a] = link
            d = d - beyond * link
        last = 1.0 / d
        inv[row + o, a] = jnp.where(inside, OMEGA * last, 0.0)
        beyond = v[row + o, a]


def rows(low, high, body, by=2):
    trips, rest = divmod(high - low, by)

    def trip(i, carry):
        for k in range(by):
            body(low + i * by + k)
        return carry

    lax.fori_loop(0, trips, trip, 0)
    for k in range(rest):
        body(low + trips * by + k)


def packed(values, of_last):
    out = jnp.zeros((SUB, LANES), F32)
    spot = lane(LANES) // EDGE
    for f, value in enumerate(values):
        shift = EDGE * f - (LANES - EDGE) if of_last else EDGE * f
        out = jnp.where(spot == f, turn(value, shift), out)
    return out


def beyond_tile(right, left, f, has_right, has_left):
    spot = lane(LANES)
    r = jnp.where(spot < has_right, turn(right, -EDGE * f), 0.0)
    return jnp.where(spot >= has_left, turn(left, LANES - EDGE - EDGE * f), r)


def limits(pos, count):
    has_right = jnp.where(pos == count - 1, 0, EDGE)
    has_left = jnp.where(pos == 0, LANES, LANES - EDGE)
    return has_right, has_left


def squeeze_row(dst, at, values):
    quarter = lane(LANES) & 3
    for i in range(BLK // 2):
        first, second = values[2 * i], values[2 * i + 1]
        out = jnp.where(quarter == 0, first[:, :LANES], first[:, LANES:])
        other = jnp.where(quarter == 2, second[:, :LANES], second[:, LANES:])
        dst[at * (BLK // 2) + i] = jnp.where(quarter < 2, out, other)


def spread_many(src, at):
    n = BLK // 2
    lanes_in = lax.broadcasted_iota(jnp.int32, (LANES, 4 * LANES), 0)
    lanes_out = lax.broadcasted_iota(jnp.int32, (LANES, 4 * LANES), 1)
    pick = ((lanes_out & (LANES - 4)) + lanes_out // LANES == lanes_in).astype(F32)
    p = src[at * n : at * n + n].reshape(n * SUB, LANES)
    full = jnp.dot(p, pick, precision=lax.Precision.HIGHEST, preferred_element_type=F32).reshape(n, SUB, 4 * LANES)
    return [full[a // 2, :, WIDE * (a % 2) : WIDE * (a % 2 + 1)] for a in LEVELS]


def spread_row(src, at):
    bits = lane(LANES)
    out = []
    for i in range(BLK // 2):
        p = src[at * (BLK // 2) + i]
        even = (bits & 1) == 0
        fill = (jnp.where(even, p, turn(p, 1)), jnp.where(even, turn(p, -1), p))
        low = (bits & 2) == 0
        for half in (0, 1):
            tiles = []
            for t in fill:
                tiles.append(jnp.where(low, t, turn(t, 2)) if half == 0 else jnp.where(low, turn(t, -2), t))
            out.append(jnp.concatenate(tiles, axis=1))
    return out


def halve_row(dst, at, values):
    even = (lane(LANES) & 1) == 0
    for a in LEVELS:
        dst[at + a] = jnp.where(even, values[a][:, :LANES], values[a][:, LANES:])


def double_row(src, at):
    even = (lane(LANES) & 1) == 0
    out = []
    for a in LEVELS:
        p = src[at + a]
        out.append(jnp.concatenate([jnp.where(even, p, turn(p, 1)), jnp.where(even, turn(p, -1), p)], axis=1))
    return out


def put(ref, at, values):
    for a in LEVELS:
        ref[at, a] = values[a]


def row_of(ref, at):
    return [ref[at, a] for a in LEVELS]


def first_kernel(*refs):
    far_in, (own, msg_a, msg_b, to_right, to_left, start), near_in, sem = refs[:6], refs[6:12], refs[12:18], refs[18]
    copies = [pltpu.make_async_copy(far_in[i], near_in[i], sem.at[i]) for i in range(6)]
    for copy in copies:
        copy.start()
    for copy in copies:
        copy.wait()
    cot, cour, ff, fs, fv, damp = near_in
    none = jnp.zeros((SUB - NBLK, LANES), F32)

    def read(ref, level, row, count=NBLK):
        got = ref[pl.ds(level * OWN + row, count, stride=BLK * OWN), :]
        if count < NBLK:
            got = jnp.concatenate([got, jnp.zeros((NBLK - count, LANES), F32)], axis=0)
        return jnp.concatenate([got, none], axis=0)

    def per_row(row, carry):
        for a in LEVELS:
            c, t = read(cour, a, row), read(cot, a, row)
            if a < BLK - 1:
                nc, nt = read(cour, a + 1, row), read(cot, a + 1, row)
                v = read(fv, a, row)
            else:
                nc, nt = read(cour, BLK, row, NBLK - 1), read(cot, BLK, row, NBLK - 1)
                v = read(fv, a, row, NBLK - 1)
            plain = read(damp, a, row)
            dl = plain + jnp.where(row > 0, read(ff, a, jnp.maximum(row - 1, 0)), 0.0)
            values = ((1.0 - c) * t + nc * nt, read(ff, a, row), read(fs, a, row), v, dl)
            for f, value in enumerate(values):
                own[row, f * BLK + a] = value
            own[row, 5 * BLK + a] = plain
            start[row, a] = values[0]
            to_right[row, a] = packed(values, True)
            to_left[row, a] = packed(values, False)
        return carry

    lax.fori_loop(0, OWN, per_row, 0)

    def per_edge(i, carry):
        for j in range(5 * BLK):
            msg_a[i, j] = own[i + OWN - DEEP, j]
            msg_b[i, j] = own[i, j]
        return carry

    lax.fori_loop(0, DEEP, per_edge, 0)


def descend(r0, x0, r1, x1, r2, c0, c1, parts=((-3, 11),)):
    (uf0, us0, m0, i0), (uf1, us1, m1, i1) = c0, c1
    for low, high in parts:
        rows(low, high, lambda row: pre(r0, x0, m0, i0, 3, row))

    def to1(coarse):
        put(r1, coarse + 2, below(r0, x0, uf0, us0, m0, 3, 1, coarse))

    rows(-1, 5, to1, 1)
    rows(-1, 5, lambda row: pre(r1, x1, m1, i1, 2, row))
    for coarse in (0, 1):
        put(r2, coarse, below(r1, x1, uf1, us1, m1, 2, 2, coarse))


def pre(r, x, m, inv, o, row):
    put(x, row + o, smooth(row_of(r, row + o), m, inv, row + o))


def below(r, x, uf, us, m, o, step, coarse):
    total = None
    for row in (2 * coarse, 2 * coarse + 1):
        near = coupled(x, o, uf, us, m, o, row, step)
        near = [near[a] + KEEP * r[row + o, a] for a in LEVELS]
        total = near if total is None else [total[a] + near[a] for a in LEVELS]
    return [pair_sum(t, step) for t in total]


def coarse_message(r1, r2, up_msg, down_msg):
    for dst, row in ((up_msg, 2), (down_msg, 1)):
        halve_row(dst, 0, row_of(r1, row + 2))
        for k in (0, 1):
            squeeze_row(dst.at[BLK:], k, row_of(r2, k))


def fill_rows(dst, o, base, count, own, edges, pos_limits, slots):
    has_right, has_left = pos_limits

    def one(i, carry):
        for a in LEVELS:
            dst[base + i + o, a, :, :LANES] = own(i, a)
            left, right = edges(i, a)
            dst[base + i + o, a, :, LANES:] = beyond_tile(right, left, slots(a), has_right, has_left)
        return carry

    lax.fori_loop(0, count, one, 0)


def inside_of(lim):
    spot = lane(WIDE)
    sub = lax.broadcasted_iota(jnp.int32, (SUB, WIDE), 0)
    return (sub < NBLK) & ((spot < LANES + lim[0]) | (spot >= LANES + lim[1]))


def ready(fields, m, inv, o, row, inside):
    uf, us, v, d = fields
    for a in LEVELS:
        d[row + o, a] = jnp.where(inside, d[row + o, a], 1.0)
    factor(uf, us, v, d, m, inv, o, row, 1, inside)


def coarsen(low, high, fine, fo, coarse, co, step, m, inv, inside):
    uf, us, v, d = fine
    cuf, cus, cv, cd = coarse

    def one(row):
        p, q = 2 * row + fo, 2 * row + 1 + fo
        for a in LEVELS:
            cuf[row + co, a] = pair_sum(uf[q, a], step)
            cus[row + co, a] = odd_of_pair(us[p, a] + us[q, a], step)
            cv[row + co, a] = pair_sum(v[p, a] + v[q, a], step)
            cd[row + co, a] = pair_sum(d[p, a] + (d[q, a] - uf[p, a]), step)
        factor(cuf, cus, cv, cd, m, inv, co, row, 2 * step, inside)

    rows(low, high, one, 1)


def face_row(low, uf, fo, cuf, co, step):
    put(cuf, low - 1 + co, [pair_sum(t, step) for t in row_of(uf, 2 * low - 1 + fo)])


def inner_kernel(count, pos, own, got_l, got_r, *refs):
    r0, x0, uf0, us0, v0, d0, m0, i0, uf1, us1, v1, d1, m1, i1 = refs
    lim = limits(pos[0], count)
    inside = inside_of(lim)
    for f, dst in enumerate((r0, uf0, us0, v0, d0)):
        fill_rows(
            dst, 0, 0, OWN, lambda i, a, f=f: own[i, f * BLK + a], lambda i, a: (got_l[i, a], got_r[i, a]), lim,
            lambda a, f=f: f,
        )
    rows(1, OWN, lambda row: ready((uf0, us0, v0, d0), m0, i0, 0, row, inside))
    coarsen(1, 4, (uf0, us0, v0, d0), 0, (uf1, us1, v1, d1), 0, 1, m1, i1, inside)
    rows(1, OWN, lambda row: pre(r0, x0, m0, i0, 0, row))


def copy_rows(dst, to, src, at, count):
    def one(i, carry):
        put(dst, to + i, row_of(src, at + i))
        return carry

    lax.fori_loop(0, count, one, 0)


def setup_kernel(count, pos, own_a, own_b, got_a, got_b, *refs):
    n_r0, n_uf0, n_us0, n_v0, n_d0, n_m0, n_i0, n_uf1, n_us1, n_v1, n_d1, n_m1, n_i1 = refs[:13]
    r0, uf0, us0, m0, i0, uf1, us1, m1, i1, uf2, us2, m2, i2 = refs[13:26]
    up_co, down_co, far_co = refs[26:29]
    v0, d0, v1, d1, v2, d2, uf3, us3, v3, d3, m3, i3 = refs[29:]
    lim = limits(pos[0], count)
    inside = inside_of(lim)
    for f, dst in enumerate((r0, uf0, us0, v0, d0)):
        for base, src, edge in ((-DEEP, own_a, got_a), (OWN, own_b, got_b)):
            edges = lambda i, a, e=edge: (e[i, a], e[i, a + BLK])
            fill_rows(dst, 3, base, DEEP, lambda i, a, s=src, f=f: s[i, f * BLK + a], edges, lim, lambda a, f=f: f)
    for dst, src in ((r0, n_r0), (uf0, n_uf0), (us0, n_us0)):
        copy_rows(dst, 3, src, 0, OWN)
    for dst, src in ((v0, n_v0), (d0, n_d0)):
        copy_rows(dst, 3, src, 0, 2)
    for dst, src in ((m0, n_m0), (i0, n_i0)):
        copy_rows(dst, 4, src, 1, OWN - 1)
    for dst, src in ((uf1, n_uf1), (us1, n_us1), (v1, n_v1), (d1, n_d1), (m1, n_m1), (i1, n_i1)):
        copy_rows(dst, 3, src, 1, 3)
    for row in (0, OWN):
        for a in LEVELS:
            d0[row + 3, a] = d0[row + 3, a] + uf0[row + 2, a]
    for low, high in ((-3, 1), (8, 11)):
        rows(low, high, lambda row: ready((uf0, us0, v0, d0), m0, i0, 3, row, inside))
    grid0, grid1, grid2 = (uf0, us0, v0, d0), (uf1, us1, v1, d1), (uf2, us2, v2, d2)
    face_row(-1, uf0, 3, uf1, 2, 1)
    for low, high in ((-1, 1), (4, 5)):
        coarsen(low, high, grid0, 3, grid1, 2, 1, m1, i1, inside)
    face_row(0, uf1, 2, uf2, 1, 2)
    coarsen(0, 2, grid1, 2, grid2, 1, 2, m2, i2, inside)
    face_row(0, uf2, 1, uf3, 1, 4)
    coarsen(0, 1, grid2, 1, (uf3, us3, v3, d3), 1, 4, m3, i3, inside)
    for dst, row in ((up_co, 2), (down_co, 1)):
        halve_row(dst, 0, row_of(m1, row + 2))
        halve_row(dst, BLK, row_of(i1, row + 2))
        at = dst.at[2 * BLK :]
        for f, ref in enumerate((m2, i2, uf2, us2)):
            for k in (0, 1):
                squeeze_row(at, 2 * f + k, row_of(ref, k + 1))
        for f, ref in enumerate((m3, i3, uf3, us3)):
            squeeze_row(at, 8 + f, row_of(ref, 1))
    for f, ref in enumerate((m3, i3, uf3, us3)):
        squeeze_row(far_co, f, row_of(ref, 1))


def outset_kernel(*refs):
    r0, x_own, c0, c1 = refs[0], refs[1], refs[2:6], refs[6:10]
    x0, r1, x1, r2, up_msg, down_msg = refs[10:]
    copy_rows(x0, 4, x_own, 1, OWN - 1)
    descend(r0, x0, r1, x1, r2, c0, c1, ((-3, 1), (8, 11)))
    coarse_message(r1, r2, up_msg, down_msg)


def coarse_kernel(uf2, us2, m2, i2, co_a, co_b, far_co, far_a, far_b, *outs):
    edge1, outs2, outs3 = outs[:2], outs[2:6], outs[6:10]
    for f in range(2):
        put(edge1[f], 0, double_row(co_a, f * BLK))
        put(edge1[f], 1, double_row(co_b, f * BLK))
    at_a, at_b = co_a.at[2 * BLK :], co_b.at[2 * BLK :]
    for f, (dst, own) in enumerate(zip(outs2, (m2, i2, uf2, us2))):
        for k in (0, 1):
            put(dst, k, spread_many(at_a, 2 * f + k))
            put(dst, k + 2, row_of(own, k + 1))
            put(dst, k + 4, spread_many(at_b, 2 * f + k))
    for f, dst in enumerate(outs3):
        put(dst, 0, spread_many(far_a, f))
        put(dst, 1, spread_many(at_a, 8 + f))
        put(dst, 2, spread_many(far_co, f))
        put(dst, 3, spread_many(at_b, 8 + f))
        put(dst, 4, spread_many(far_b, f))


def again_kernel(count, pos, own, got_l, got_r, all_a, all_b, *refs):
    c0, c1 = refs[:4], refs[4:8]
    r0, x0, r1, x1, r2, up_msg, down_msg = refs[8:]
    lim = limits(pos[0], count)
    slots = lambda a: a % PACK
    fill_rows(
        r0, 3, 0, OWN, lambda i, a: own[i, a],
        lambda i, a: (got_l[i, a // PACK], got_r[i, a // PACK]), lim, slots,
    )
    for base, src in ((-DEEP, all_a), (OWN, all_b)):
        fill_rows(
            r0, 3, base, DEEP, lambda i, a, s=src: s[i, a],
            lambda i, a, s=src: (s[i, BLK + a // PACK], s[i, BLK + 2 + a // PACK]), lim, slots,
        )
    descend(r0, x0, r1, x1, r2, c0, c1)
    coarse_message(r1, r2, up_msg, down_msg)


def middle_kernel(r2_own, got_a, got_b, m2, i2, uf2, us2, r2, x2, r3, msg):
    for k in (0, 1):
        put(r2, k, spread_row(got_a.at[BLK:], k))
        put(r2, k + 2, row_of(r2_own, k))
        put(r2, k + 4, spread_row(got_b.at[BLK:], k))
    rows(-2, 4, lambda row: pre(r2, x2, m2, i2, 2, row))
    got = below(r2, x2, uf2, us2, m2, 2, 4, 0)
    put(r3, 0, got)
    squeeze_row(msg, 0, got)


def ascend_kernel(number, *refs):
    refs = list(refs)
    take = lambda n: [refs.pop(0) for _ in range(n)]
    r_own, own, got_a, got_b, r3_own, near_a, near_b, far_a, far_b = take(9)
    r0, x0_in, r1_in, x1_in, r2, x2_in = take(6)
    uf0, us0, m0, i0 = take(4)
    uf1, us1, m1, i1, m1_edge, i1_edge = take(6)
    m2, i2, uf2, us2, m3, i3, uf3, us3 = take(8)
    past = []
    if number == 2:
        past = take(5)
        first_r = take(1)[0]
    z_own, w_own = take(2)
    if number < 2:
        r_next, to_right, to_left = take(3)
    else:
        gram = take(1)[0]
    x2, r3, x3, e3, e2, e1, z0, x1, x0, r_edge = take(10)

    put(r3, 0, spread_row(far_a, 0))
    put(r3, 1, spread_row(near_a, 0))
    put(r3, 2, row_of(r3_own, 0))
    put(r3, 3, spread_row(near_b, 0))
    put(r3, 4, spread_row(far_b, 0))
    rows(0, 5, lambda at: pre(r3, x3, m3, i3, 0, at))

    def post(r, x, uf, us, m, inv, o, step, row):
        near_x = coupled(x, 2, uf, us, m, o, row, step)
        got = smooth([near_x[a] + r[row + o, a] for a in LEVELS], m, inv, row + o)
        return [got[a] + KEEP * x[row + 2, a] for a in LEVELS]

    for row in (-1, 0, 1):
        put(e3, row + 1, post(r3, x3, uf3, us3, m3, i3, 2, 8, row))
    put(r_edge, 0, double_row(got_a, 0))
    put(r_edge, 1, double_row(got_b, 0))

    def add(dst, do, x, o, e, coarse):
        for row in (2 * coarse, 2 * coarse + 1):
            for a in LEVELS:
                dst[row + do, a] = x[row + o, a] + e[coarse + 1, a]

    rows(-1, 2, lambda c: add(x2, 2, x2_in, 2, e3, c), 1)
    rows(-1, 3, lambda row: put(e2, row + 1, post(r2, x2, uf2, us2, m2, i2, 2, 4, row)))
    rows(0, 2, lambda c: add(x1, 2, x1_in, 2, e2, c), 1)
    for at, row, coarse in ((0, -2, -1), (1, 5, 2)):
        outer = smooth(row_of(r_edge, at), m1_edge, i1_edge, at)
        inner = row_of(x1_in, (-1 if at == 0 else 4) + 2)
        for a in LEVELS:
            x1[row + 2, a] = outer[a] + e2[coarse + 1, a]
            x1[(-1 if at == 0 else 4) + 2, a] = inner[a] + e2[coarse + 1, a]
    rows(-1, 5, lambda row: put(e1, row + 1, post(r1_in, x1, uf1, us1, m1, i1, 2, 2, row)))
    rows(-1, 5, lambda c: add(x0, 2, x0_in, 3, e1, c), 1)
    rows(-1, 9, lambda row: put(z0, row + 1, post(r0, x0, uf0, us0, m0, i0, 3, 1, row)))

    def image(row):
        flux = None
        last = z0[row + 1, BLK - 1][:, :LANES]
        first_z = z0[row + 1, 0][:, :LANES]
        over = own[row, 3 * BLK + BLK - 1] * (up(first_z) - last)
        below = down(over)
        for a in LEVELS:
            wide = z0[row + 1, a]
            here = wide[:, :LANES]
            side = us0[row + 3, a] * (wide - turn(wide, -1))
            total = own[row, 5 * BLK + a] * here + (side - turn(side, 1))[:, :LANES]
            total = total + uf0[row + 3, a][:, :LANES] * (here - z0[row + 2, a][:, :LANES])
            total = total + uf0[row + 2, a][:, :LANES] * (here - z0[row, a][:, :LANES])
            if a < BLK - 1:
                flux = own[row, 3 * BLK + a] * (z0[row + 1, a + 1][:, :LANES] - here)
            else:
                flux = over
            total = total - flux + below
            below = flux
            w_own[row, a] = total
            z_own[row, a] = here
            if number < 2:
                r_next[row, a] = r_own[row, a] - THETA * total
        if number < 2:
            for g in range(BLK // PACK):
                values = [r_next[row, g * PACK + f] for f in range(PACK)]
                to_right[row, g] = packed(values, True)
                to_left[row, g] = packed(values, False)

    rows(0, OWN, image, 1)

    if number == 2:
        g_r0, g_z0, g_w0, g_z1, g_w1 = past

        def dots(row, acc):
            acc = list(acc)
            for a in LEVELS:
                z = (g_z0[row, a], g_z1[row, a], z_own[row, a])
                w = (g_w0[row, a], g_w1[row, a], w_own[row, a])
                r = (g_r0[row, a], first_r[row, a], r_own[row, a])
                terms = [r[i] * z[j] for i in range(3) for j in range(i + 1)]
                terms += [w[i] * z[j] for i in range(3) for j in range(3)]
                acc = [s + t for s, t in zip(acc, terms)]
            return tuple(acc)

        acc = lax.fori_loop(0, OWN, dots, tuple(jnp.zeros((SUB, LANES), F32) for _ in range(15)))
        gram[...] = jnp.zeros_like(gram)
        for i in range(15):
            gram[i : i + 1, :] = jnp.sum(acc[i], axis=0, keepdims=True)


def last_kernel(gram, r2, z0, z1, z2, w0, w1, w2, sol, res):
    get = lambda i: jnp.broadcast_to(jnp.sum(gram[i : i + 1, :], axis=1, keepdims=True), (SUB, LANES))
    q, at = {}, 0
    for i in range(3):
        for j in range(i + 1):
            q["r", i, j] = get(at)
            at += 1
    for i in range(3):
        for j in range(3):
            q["w", i, j] = get(at)
            at += 1
    zero = jnp.zeros((SUB, LANES), F32)

    def product(base, c, z):
        total = zero
        for j in range(3):
            if z[j] is None:
                continue
            term = q["r", base, j] if base is not None else zero
            for i in range(3):
                if c[i] is not None:
                    term = term + c[i] * q["w", i, j]
            total = total + z[j] * term
        return total

    one = zero + 1.0
    c = [None] * 3
    p = [one, None, None]
    gamma = q["r", 0, 0]
    x = [zero] * 3
    plus = lambda s, t: t if s is None else s + t
    for step in range(3):
        alpha = gamma / product(None, p, p)
        for j in range(step + 1):
            x[j] = x[j] + alpha * p[j]
            c[j] = plus(c[j], -(alpha * p[j]))
        if step == 2:
            break
        c[step] = c[step] + THETA
        z = [None] * 3
        z[step + 1] = one
        for i in range(step + 1):
            part = c[i] * (1.0 / THETA)
            z[i] = plus(z[i], part)
            z[i + 1] = plus(z[i + 1], -part)
        fresh = product(step + 1, c, z)
        beta = fresh / gamma
        p = [plus(z[j], beta * p[j]) if p[j] is not None else z[j] for j in range(3)]
        gamma = fresh

    def per_row(row, carry):
        for a in LEVELS:
            s = x[0] * z0[row, a] + x[1] * z1[row, a] + x[2] * z2[row, a]
            t = r2[row, a] + c[0] * w0[row, a] + c[1] * w1[row, a] + c[2] * w2[row, a]
            sol[pl.ds(a * OWN + row, NBLK, stride=BLK * OWN), :] = s[:NBLK]
            res[pl.ds(a * OWN + row, NBLK, stride=BLK * OWN), :] = t[:NBLK]
        return carry

    lax.fori_loop(0, OWN, per_row, 0)


def per_device(cotangent, courant, faces_first, faces_second, faces_vertical, damping, *blocks):
    n_rows = lax.axis_size(ROWS_AX)
    n_cols = lax.axis_size(COLS_AX)
    pos = lax.axis_index(COLS_AX).reshape(1).astype(jnp.int32)

    def send(x, dr, dc):
        route = [
            (r * n_cols + c, ((r + dr) % n_rows) * n_cols + (c + dc) % n_cols)
            for r in range(n_rows)
            for c in range(n_cols)
        ]
        return lax.ppermute(x, ALL, route)

    def total_over(x, axis):
        size, done = lax.axis_size(axis), 1
        while done < size:
            count = 4 if size // done >= 4 else 2
            route = lambda by: [(i, (i + by) % size) for i in range(size)]
            shifts = (1, 2, -1)[: count - 1] if count == 4 else (1,)
            x = functools.reduce(jnp.add, [lax.ppermute(x, axis, route(k * done)) for k in shifts], x)
            done *= count
        return x

    flat = lambda x: x.reshape(x.shape[0] * OWN, LANES)
    wide = lambda n: shape(n, BLK, SUB, WIDE)
    tile = lambda *n: shape(*n, SUB, LANES)
    vwide = lambda n: pltpu.VMEM((n, BLK, SUB, WIDE), F32)

    own, msg_a, msg_b, to_right, to_left, start = pl.pallas_call(
        first_kernel,
        out_shape=[
            tile(OWN, 6 * BLK), tile(DEEP, 5 * BLK), tile(DEEP, 5 * BLK),
            tile(OWN, BLK), tile(OWN, BLK), tile(OWN, BLK),
        ],
        in_specs=[pl.BlockSpec(memory_space=pltpu.HBM)] * 6,
        out_specs=[VM] * 6,
        scratch_shapes=[pltpu.VMEM(((LEV - (i == 4)) * OWN, LANES), F32) for i in range(6)]
        + [pltpu.SemaphoreType.DMA((6,))],
        compiler_params=params(),
    )(*[pltpu.with_memory_space_constraint(flat(x), pltpu.HBM) for x in (cotangent, courant, faces_first, faces_second, faces_vertical, damping)])
    own_a, own_b = send(msg_a, 1, 0), send(msg_b, -1, 0)
    got_l, got_r = send(to_right, 0, 1), send(to_left, 0, -1)
    got_a = send(jnp.concatenate([got_l[-DEEP:], got_r[-DEEP:]], axis=1), 1, 0)
    got_b = send(jnp.concatenate([got_l[:DEEP], got_r[:DEEP]], axis=1), -1, 0)

    inner = call(
        functools.partial(inner_kernel, n_cols),
        [wide(8)] * 8 + [wide(4)] * 6,
        [pos, own, got_l, got_r],
    )
    x_own, inner = inner[1], [inner[0], *inner[2:]]
    outs = call(
        functools.partial(setup_kernel, n_cols),
        [wide(14)] * 5 + [wide(8)] * 4 + [wide(3)] * 4 + [tile(80)] * 2 + [tile(20)],
        [pos, own_a, own_b, got_a, got_b, *inner],
        [vwide(n) for n in (14, 14, 8, 8, 3, 3, 3, 3, 3, 3, 3, 3)],
    )
    r0, uf0, us0, m0, i0, uf1, us1, m1, i1, uf2, us2, m2, i2, up_co, down_co, far_co = outs
    c0, c1 = (uf0, us0, m0, i0), (uf1, us1, m1, i1)
    co_a, co_b = send(up_co, 1, 0), send(down_co, -1, 0)
    far_a, far_b = send(far_co, 2, 0), send(far_co, -2, 0)
    x0, r1, x1, r2, up_msg, down_msg = call(
        outset_kernel,
        [wide(14), wide(8), wide(8), wide(2), tile(20), tile(20)],
        [r0, x_own, *c0, *c1],
    )
    residuals, zs, ws = [start], [], []
    upward = [vwide(n) for n in (6, 5, 5, 3, 4, 6, 10, 8, 12, 2)]
    for number in range(3):
        if number:
            got_l, got_r = send(to_right, 0, 1), send(to_left, 0, -1)
            whole = jnp.concatenate([residuals[-1], got_l, got_r], axis=1)
            all_a, all_b = send(whole[OWN - DEEP :], 1, 0), send(whole[:DEEP], -1, 0)
            r0, x0, r1, x1, r2, up_msg, down_msg = call(
                functools.partial(again_kernel, n_cols),
                [wide(14)] * 2 + [wide(8)] * 2 + [wide(2)] + [tile(20)] * 2,
                [pos, residuals[-1], got_l, got_r, all_a, all_b, *c0, *c1],
            )
        msg_a, msg_b = send(up_msg, 1, 0), send(down_msg, -1, 0)
        if number == 0:
            coarse = call(
                coarse_kernel,
                [wide(2)] * 2 + [wide(6)] * 4 + [wide(5)] * 4,
                [uf2, us2, m2, i2, co_a, co_b, far_co, far_a, far_b],
            )
            edge1, c2, c3 = coarse[:2], coarse[2:6], coarse[6:]
        r2, x2, r3, msg = call(
            middle_kernel,
            [wide(6)] * 2 + [wide(1), tile(5)],
            [r2, msg_a, msg_b, *c2],
        )
        near_a, near_b = send(msg, 1, 0), send(msg, -1, 0)
        far_a, far_b = send(msg, 2, 0), send(msg, -2, 0)
        ins = [residuals[-1], own, msg_a, msg_b, r3, near_a, near_b, far_a, far_b, r0, x0, r1, x1, r2, x2]
        ins += [*c0, *c1, *edge1, *c2, *c3]
        if number == 2:
            ins += [residuals[0], zs[0], ws[0], zs[1], ws[1], residuals[1]]
        outs = [tile(OWN, BLK)] * 2
        outs += [tile(OWN, BLK), tile(OWN, 2), tile(OWN, 2)] if number < 2 else [shape(16, LANES)]
        outs = call(functools.partial(ascend_kernel, number), outs, ins, upward)
        zs.append(outs[0])
        ws.append(outs[1])
        if number < 2:
            residuals.append(outs[2])
            to_right, to_left = outs[3:]
        else:
            gram = outs[2]
    for axis in (COLS_AX, "tx", "panel"):
        gram = total_over(gram, axis)
    sol, res = call(
        last_kernel,
        [shape(LEV * OWN, LANES)] * 2,
        [gram, residuals[2], *zs, *ws],
    )
    return sol.reshape(LEV, OWN, LANES), res.reshape(LEV, OWN, LANES)


def solution(mesh):
    field = P(None, ROWS_AX, COLS_AX)
    block = P(None, None, None, ROWS_AX, COLS_AX)
    return jax.shard_map(
        per_device,
        mesh=mesh,
        in_specs=(field,) * 6 + (block,) * 4,
        out_specs=(field, field),
        check_vma=False,
    )
```

```python
import functools

import jax
import jax.numpy as jnp
from jax import lax
from jax.experimental import pallas as pl
from jax.experimental.pallas import tpu as pltpu
from jax.sharding import PartitionSpec as P

ROWS_AX = ("panel", "tx")
COLS_AX = "ty"
ALL = ("panel", "tx", "ty")

LEV = 70
BLK = 10
NBLK = 7
SUB = 8
OWN = 8
LANES = 128
WIDE = 256
EDGE = 24
PACK = 5
DEEP = 3
OMEGA = 0.8
KEEP = 1.0 - OMEGA
THETA = 1.0

F32 = jnp.float32
VM = pl.BlockSpec(memory_space=pltpu.VMEM)
SM = pl.BlockSpec(memory_space=pltpu.SMEM)
LEVELS = tuple(range(BLK))


def params():
    return pltpu.CompilerParams(vmem_limit_bytes=12 << 20)


def shape(*dims):
    return jax.ShapeDtypeStruct(dims, F32)


def call(body, outs, ins, scratch=()):
    specs = [SM if x.dtype == jnp.int32 else VM for x in ins]
    return pl.pallas_call(
        body,
        out_shape=list(outs),
        in_specs=specs,
        out_specs=[VM] * len(outs),
        scratch_shapes=list(scratch),
        compiler_params=params(),
        cost_estimate=pl.CostEstimate(flops=8_000_000, bytes_accessed=16_000_000, transcendentals=0),
    )(*ins)


def lane(width):
    return lax.broadcasted_iota(jnp.int32, (SUB, width), 1)


def turn(x, by):
    return pltpu.roll(x, by % x.shape[1], 1)


def down(x):
    return pltpu.roll(x, 1, 0)


def up(x):
    return pltpu.roll(x, SUB - 1, 0)


def pair_sum(x, step):
    bit = (lane(x.shape[1]) & step) == 0
    return x + jnp.where(bit, turn(x, -step), turn(x, step))


def odd_of_pair(x, step):
    bit = (lane(x.shape[1]) & step) == 0
    return jnp.where(bit, turn(x, -step), x)


def smooth(rhs, m, inv, at):
    y = [rhs[0]]
    for a in LEVELS[1:]:
        y.append(rhs[a] + m[at, a] * y[a - 1])
    x = [None] * BLK
    x[BLK - 1] = y[BLK - 1] * inv[at, BLK - 1]
    for a in LEVELS[-2::-1]:
        x[a] = y[a] * inv[at, a] + m[at, a + 1] * x[a + 1]
    return x


def coupled(x, xo, uf, us, m, co, row, step):
    out = []
    for a in LEVELS:
        here = x[row + xo, a]
        flow = us[row + co, a] * turn(here, -step) + turn(us[row + co, a] * here, step)
        flow = flow + uf[row + co, a] * x[row + xo + 1, a]
        flow = flow + uf[row + co - 1, a] * x[row + xo - 1, a]
        out.append(flow)
    edge = m[row + co, 0]
    out[0] = out[0] + down(edge * x[row + xo, BLK - 1])
    out[BLK - 1] = out[BLK - 1] + edge * up(x[row + xo, 0])
    return out


def factor(uf, us, v, dl, m, inv, o, row, step, inside):
    m[row + o, 0] = v[row + o, BLK - 1]
    beyond = down(v[row + o, BLK - 1])
    last = None
    for a in LEVELS:
        d = dl[row + o, a] + uf[row + o, a] + us[row + o, a]
        d = d + turn(us[row + o, a], step) + v[row + o, a] + beyond
        if a:
            link = beyond * last
            m[row + o, a] = link
            d = d - beyond * link
        last = 1.0 / d
        inv[row + o, a] = jnp.where(inside, OMEGA * last, 0.0)
        beyond = v[row + o, a]


def rows(low, high, body, by=2):
    trips, rest = divmod(high - low, by)

    def trip(i, carry):
        for k in range(by):
            body(low + i * by + k)
        return carry

    lax.fori_loop(0, trips, trip, 0)
    for k in range(rest):
        body(low + trips * by + k)


def packed(values, of_last):
    out = jnp.zeros((SUB, LANES), F32)
    spot = lane(LANES) // EDGE
    for f, value in enumerate(values):
        shift = EDGE * f - (LANES - EDGE) if of_last else EDGE * f
        out = jnp.where(spot == f, turn(value, shift), out)
    return out


def beyond_tile(right, left, f, has_right, has_left):
    spot = lane(LANES)
    r = jnp.where(spot < has_right, turn(right, -EDGE * f), 0.0)
    return jnp.where(spot >= has_left, turn(left, LANES - EDGE - EDGE * f), r)


def limits(pos, count):
    has_right = jnp.where(pos == count - 1, 0, EDGE)
    has_left = jnp.where(pos == 0, LANES, LANES - EDGE)
    return has_right, has_left


def squeeze_row(dst, at, values):
    quarter = lane(LANES) & 3
    for i in range(BLK // 2):
        first, second = values[2 * i], values[2 * i + 1]
        out = jnp.where(quarter == 0, first[:, :LANES], first[:, LANES:])
        other = jnp.where(quarter == 2, second[:, :LANES], second[:, LANES:])
        dst[at * (BLK // 2) + i] = jnp.where(quarter < 2, out, other)


def spread_many(src, at):
    n = BLK // 2
    lanes_in = lax.broadcasted_iota(jnp.int32, (LANES, 4 * LANES), 0)
    lanes_out = lax.broadcasted_iota(jnp.int32, (LANES, 4 * LANES), 1)
    pick = ((lanes_out & (LANES - 4)) + lanes_out // LANES == lanes_in).astype(F32)
    p = src[at * n : at * n + n].reshape(n * SUB, LANES)
    full = jnp.dot(p, pick, precision=lax.Precision.HIGHEST, preferred_element_type=F32).reshape(n, SUB, 4 * LANES)
    return [full[a // 2, :, WIDE * (a % 2) : WIDE * (a % 2 + 1)] for a in LEVELS]


def spread_row(src, at):
    bits = lane(LANES)
    out = []
    for i in range(BLK // 2):
        p = src[at * (BLK // 2) + i]
        even = (bits & 1) == 0
        fill = (jnp.where(even, p, turn(p, 1)), jnp.where(even, turn(p, -1), p))
        low = (bits & 2) == 0
        for half in (0, 1):
            tiles = []
            for t in fill:
                tiles.append(jnp.where(low, t, turn(t, 2)) if half == 0 else jnp.where(low, turn(t, -2), t))
            out.append(jnp.concatenate(tiles, axis=1))
    return out


def halve_row(dst, at, values):
    even = (lane(LANES) & 1) == 0
    for a in LEVELS:
        dst[at + a] = jnp.where(even, values[a][:, :LANES], values[a][:, LANES:])


def double_row(src, at):
    even = (lane(LANES) & 1) == 0
    out = []
    for a in LEVELS:
        p = src[at + a]
        out.append(jnp.concatenate([jnp.where(even, p, turn(p, 1)), jnp.where(even, turn(p, -1), p)], axis=1))
    return out


def put(ref, at, values):
    for a in LEVELS:
        ref[at, a] = values[a]


def row_of(ref, at):
    return [ref[at, a] for a in LEVELS]


def first_kernel(*refs):
    far_in, (own, msg_a, msg_b, to_right, to_left, start), near_in, sem = refs[:6], refs[6:12], refs[12:18], refs[18]
    copies = [pltpu.make_async_copy(far_in[i], near_in[i], sem.at[i]) for i in range(6)]
    for copy in copies:
        copy.start()
    for copy in copies:
        copy.wait()
    cot, cour, ff, fs, fv, damp = near_in
    none = jnp.zeros((SUB - NBLK, LANES), F32)

    def read(ref, level, row, count=NBLK):
        got = ref[pl.ds(level * OWN + row, count, stride=BLK * OWN), :]
        if count < NBLK:
            got = jnp.concatenate([got, jnp.zeros((NBLK - count, LANES), F32)], axis=0)
        return jnp.concatenate([got, none], axis=0)

    def per_row(row, carry):
        for a in LEVELS:
            c, t = read(cour, a, row), read(cot, a, row)
            if a < BLK - 1:
                nc, nt = read(cour, a + 1, row), read(cot, a + 1, row)
                v = read(fv, a, row)
            else:
                nc, nt = read(cour, BLK, row, NBLK - 1), read(cot, BLK, row, NBLK - 1)
                v = read(fv, a, row, NBLK - 1)
            plain = read(damp, a, row)
            dl = plain + jnp.where(row > 0, read(ff, a, jnp.maximum(row - 1, 0)), 0.0)
            values = ((1.0 - c) * t + nc * nt, read(ff, a, row), read(fs, a, row), v, dl)
            for f, value in enumerate(values):
                own[row, f * BLK + a] = value
            own[row, 5 * BLK + a] = plain
            start[row, a] = values[0]
            to_right[row, a] = packed(values, True)
            to_left[row, a] = packed(values, False)
        return carry

    lax.fori_loop(0, OWN, per_row, 0)

    def per_edge(i, carry):
        for j in range(5 * BLK):
            msg_a[i, j] = own[i + OWN - DEEP, j]
            msg_b[i, j] = own[i, j]
        return carry

    lax.fori_loop(0, DEEP, per_edge, 0)


def descend(r0, x0, r1, x1, r2, c0, c1, parts=((-3, 11),)):
    (uf0, us0, m0, i0), (uf1, us1, m1, i1) = c0, c1
    for low, high in parts:
        rows(low, high, lambda row: pre(r0, x0, m0, i0, 3, row))

    def to1(coarse):
        put(r1, coarse + 2, below(r0, x0, uf0, us0, m0, 3, 1, coarse))

    rows(-1, 5, to1, 1)
    rows(-1, 5, lambda row: pre(r1, x1, m1, i1, 2, row))
    for coarse in (0, 1):
        put(r2, coarse, below(r1, x1, uf1, us1, m1, 2, 2, coarse))


def pre(r, x, m, inv, o, row):
    put(x, row + o, smooth(row_of(r, row + o), m, inv, row + o))


def below(r, x, uf, us, m, o, step, coarse):
    total = None
    for row in (2 * coarse, 2 * coarse + 1):
        near = coupled(x, o, uf, us, m, o, row, step)
        near = [near[a] + KEEP * r[row + o, a] for a in LEVELS]
        total = near if total is None else [total[a] + near[a] for a in LEVELS]
    return [pair_sum(t, step) for t in total]


def coarse_message(r1, r2, up_msg, down_msg):
    for dst, row in ((up_msg, 2), (down_msg, 1)):
        halve_row(dst, 0, row_of(r1, row + 2))
        for k in (0, 1):
            squeeze_row(dst.at[BLK:], k, row_of(r2, k))


def fill_rows(dst, o, base, count, own, edges, pos_limits, slots):
    has_right, has_left = pos_limits

    def one(i, carry):
        for a in LEVELS:
            dst[base + i + o, a, :, :LANES] = own(i, a)
            left, right = edges(i, a)
            dst[base + i + o, a, :, LANES:] = beyond_tile(right, left, slots(a), has_right, has_left)
        return carry

    lax.fori_loop(0, count, one, 0)


def inside_of(lim):
    spot = lane(WIDE)
    sub = lax.broadcasted_iota(jnp.int32, (SUB, WIDE), 0)
    return (sub < NBLK) & ((spot < LANES + lim[0]) | (spot >= LANES + lim[1]))


def ready(fields, m, inv, o, row, inside):
    uf, us, v, d = fields
    for a in LEVELS:
        d[row + o, a] = jnp.where(inside, d[row + o, a], 1.0)
    factor(uf, us, v, d, m, inv, o, row, 1, inside)


def coarsen(low, high, fine, fo, coarse, co, step, m, inv, inside):
    uf, us, v, d = fine
    cuf, cus, cv, cd = coarse

    def one(row):
        p, q = 2 * row + fo, 2 * row + 1 + fo
        for a in LEVELS:
            cuf[row + co, a] = pair_sum(uf[q, a], step)
            cus[row + co, a] = odd_of_pair(us[p, a] + us[q, a], step)
            cv[row + co, a] = pair_sum(v[p, a] + v[q, a], step)
            cd[row + co, a] = pair_sum(d[p, a] + (d[q, a] - uf[p, a]), step)
        factor(cuf, cus, cv, cd, m, inv, co, row, 2 * step, inside)

    rows(low, high, one, 1)


def face_row(low, uf, fo, cuf, co, step):
    put(cuf, low - 1 + co, [pair_sum(t, step) for t in row_of(uf, 2 * low - 1 + fo)])


def inner_kernel(count, pos, own, got_l, got_r, *refs):
    r0, x0, uf0, us0, v0, d0, m0, i0, uf1, us1, v1, d1, m1, i1 = refs
    lim = limits(pos[0], count)
    inside = inside_of(lim)
    for f, dst in enumerate((r0, uf0, us0, v0, d0)):
        fill_rows(
            dst, 0, 0, OWN, lambda i, a, f=f: own[i, f * BLK + a], lambda i, a: (got_l[i, a], got_r[i, a]), lim,
            lambda a, f=f: f,
        )
    rows(1, OWN, lambda row: ready((uf0, us0, v0, d0), m0, i0, 0, row, inside))
    coarsen(1, 4, (uf0, us0, v0, d0), 0, (uf1, us1, v1, d1), 0, 1, m1, i1, inside)
    rows(1, OWN, lambda row: pre(r0, x0, m0, i0, 0, row))


def copy_rows(dst, to, src, at, count):
    def one(i, carry):
        put(dst, to + i, row_of(src, at + i))
        return carry

    lax.fori_loop(0, count, one, 0)


def setup_kernel(count, pos, own_a, own_b, got_a, got_b, *refs):
    n_r0, n_uf0, n_us0, n_v0, n_d0, n_m0, n_i0, n_uf1, n_us1, n_v1, n_d1, n_m1, n_i1 = refs[:13]
    r0, uf0, us0, m0, i0, uf1, us1, m1, i1, uf2, us2, m2, i2 = refs[13:26]
    up_co, down_co, far_co = refs[26:29]
    v0, d0, v1, d1, v2, d2, uf3, us3, v3, d3, m3, i3 = refs[29:]
    lim = limits(pos[0], count)
    inside = inside_of(lim)
    for f, dst in enumerate((r0, uf0, us0, v0, d0)):
        for base, src, edge in ((-DEEP, own_a, got_a), (OWN, own_b, got_b)):
            edges = lambda i, a, e=edge: (e[i, a], e[i, a + BLK])
            fill_rows(dst, 3, base, DEEP, lambda i, a, s=src, f=f: s[i, f * BLK + a], edges, lim, lambda a, f=f: f)
    for dst, src in ((r0, n_r0), (uf0, n_uf0), (us0, n_us0)):
        copy_rows(dst, 3, src, 0, OWN)
    for dst, src in ((v0, n_v0), (d0, n_d0)):
        copy_rows(dst, 3, src, 0, 2)
    for dst, src in ((m0, n_m0), (i0, n_i0)):
        copy_rows(dst, 4, src, 1, OWN - 1)
    for dst, src in ((uf1, n_uf1), (us1, n_us1), (v1, n_v1), (d1, n_d1), (m1, n_m1), (i1, n_i1)):
        copy_rows(dst, 3, src, 1, 3)
    for row in (0, OWN):
        for a in LEVELS:
            d0[row + 3, a] = d0[row + 3, a] + uf0[row + 2, a]
    for low, high in ((-3, 1), (8, 11)):
        rows(low, high, lambda row: ready((uf0, us0, v0, d0), m0, i0, 3, row, inside))
    grid0, grid1, grid2 = (uf0, us0, v0, d0), (uf1, us1, v1, d1), (uf2, us2, v2, d2)
    face_row(-1, uf0, 3, uf1, 2, 1)
    for low, high in ((-1, 1), (4, 5)):
        coarsen(low, high, grid0, 3, grid1, 2, 1, m1, i1, inside)
    face_row(0, uf1, 2, uf2, 1, 2)
    coarsen(0, 2, grid1, 2, grid2, 1, 2, m2, i2, inside)
    face_row(0, uf2, 1, uf3, 1, 4)
    coarsen(0, 1, grid2, 1, (uf3, us3, v3, d3), 1, 4, m3, i3, inside)
    for dst, row in ((up_co, 2), (down_co, 1)):
        halve_row(dst, 0, row_of(m1, row + 2))
        halve_row(dst, BLK, row_of(i1, row + 2))
        at = dst.at[2 * BLK :]
        for f, ref in enumerate((m2, i2, uf2, us2)):
            for k in (0, 1):
                squeeze_row(at, 2 * f + k, row_of(ref, k + 1))
        for f, ref in enumerate((m3, i3, uf3, us3)):
            squeeze_row(at, 8 + f, row_of(ref, 1))
    for f, ref in enumerate((m3, i3, uf3, us3)):
        squeeze_row(far_co, f, row_of(ref, 1))


def outset_kernel(*refs):
    r0, x_own, c0, c1 = refs[0], refs[1], refs[2:6], refs[6:10]
    x0, r1, x1, r2, up_msg, down_msg = refs[10:]
    copy_rows(x0, 4, x_own, 1, OWN - 1)
    descend(r0, x0, r1, x1, r2, c0, c1, ((-3, 1), (8, 11)))
    coarse_message(r1, r2, up_msg, down_msg)


def coarse_kernel(uf2, us2, m2, i2, co_a, co_b, far_co, far_a, far_b, *outs):
    edge1, outs2, outs3 = outs[:2], outs[2:6], outs[6:10]
    for f in range(2):
        put(edge1[f], 0, double_row(co_a, f * BLK))
        put(edge1[f], 1, double_row(co_b, f * BLK))
    at_a, at_b = co_a.at[2 * BLK :], co_b.at[2 * BLK :]
    for f, (dst, own) in enumerate(zip(outs2, (m2, i2, uf2, us2))):
        for k in (0, 1):
            put(dst, k, spread_many(at_a, 2 * f + k))
            put(dst, k + 2, row_of(own, k + 1))
            put(dst, k + 4, spread_many(at_b, 2 * f + k))
    for f, dst in enumerate(outs3):
        put(dst, 0, spread_many(far_a, f))
        put(dst, 1, spread_many(at_a, 8 + f))
        put(dst, 2, spread_many(far_co, f))
        put(dst, 3, spread_many(at_b, 8 + f))
        put(dst, 4, spread_many(far_b, f))


def again_kernel(count, pos, own, got_l, got_r, all_a, all_b, *refs):
    c0, c1 = refs[:4], refs[4:8]
    r0, x0, r1, x1, r2, up_msg, down_msg = refs[8:]
    lim = limits(pos[0], count)
    slots = lambda a: a % PACK
    fill_rows(
        r0, 3, 0, OWN, lambda i, a: own[i, a],
        lambda i, a: (got_l[i, a // PACK], got_r[i, a // PACK]), lim, slots,
    )
    for base, src in ((-DEEP, all_a), (OWN, all_b)):
        fill_rows(
            r0, 3, base, DEEP, lambda i, a, s=src: s[i, a],
            lambda i, a, s=src: (s[i, BLK + a // PACK], s[i, BLK + 2 + a // PACK]), lim, slots,
        )
    descend(r0, x0, r1, x1, r2, c0, c1)
    coarse_message(r1, r2, up_msg, down_msg)


def middle_kernel(r2_own, got_a, got_b, m2, i2, uf2, us2, r2, x2, r3, msg):
    for k in (0, 1):
        put(r2, k, spread_row(got_a.at[BLK:], k))
        put(r2, k + 2, row_of(r2_own, k))
        put(r2, k + 4, spread_row(got_b.at[BLK:], k))
    rows(-2, 4, lambda row: pre(r2, x2, m2, i2, 2, row))
    got = below(r2, x2, uf2, us2, m2, 2, 4, 0)
    put(r3, 0, got)
    squeeze_row(msg, 0, got)


def join_kernel(first, second, both):
    half = first.shape[0]
    both[:half] = first[...]
    both[half:] = second[...]


def ascend_kernel(number, *refs):
    refs = list(refs)
    take = lambda n: [refs.pop(0) for _ in range(n)]
    odd, r_own, own, got_a, got_b, r3_own, mate, before, after = take(9)
    r0, x0_in, r1_in, x1_in, r2, x2_in = take(6)
    uf0, us0, m0, i0 = take(4)
    uf1, us1, m1, i1, m1_edge, i1_edge = take(6)
    m2, i2, uf2, us2, m3, i3, uf3, us3 = take(8)
    past = []
    if number == 2:
        past = take(5)
        first_r = take(1)[0]
    z_own, w_own = take(2)
    if number < 2:
        r_next, to_right, to_left = take(3)
    else:
        gram = take(1)[0]
    x2, r3, x3, e3, e2, e1, z0, x1, x0, r_edge, near = take(11)

    half = BLK // 2
    for i in range(half):
        near[i] = jnp.where(odd[1] == 1, mate[i], before[half + i])
        near[half + i] = jnp.where(odd[1] == 1, after[half + i], mate[i])
    put(r3, 0, spread_row(before, 0))
    put(r3, 1, spread_row(near, 0))
    put(r3, 2, row_of(r3_own, 0))
    put(r3, 3, spread_row(near, 1))
    put(r3, 4, spread_row(after, 0))
    rows(0, 5, lambda at: pre(r3, x3, m3, i3, 0, at))

    def post(r, x, uf, us, m, inv, o, step, row):
        near_x = coupled(x, 2, uf, us, m, o, row, step)
        got = smooth([near_x[a] + r[row + o, a] for a in LEVELS], m, inv, row + o)
        return [got[a] + KEEP * x[row + 2, a] for a in LEVELS]

    for row in (-1, 0, 1):
        put(e3, row + 1, post(r3, x3, uf3, us3, m3, i3, 2, 8, row))
    put(r_edge, 0, double_row(got_a, 0))
    put(r_edge, 1, double_row(got_b, 0))

    def add(dst, do, x, o, e, coarse):
        for row in (2 * coarse, 2 * coarse + 1):
            for a in LEVELS:
                dst[row + do, a] = x[row + o, a] + e[coarse + 1, a]

    rows(-1, 2, lambda c: add(x2, 2, x2_in, 2, e3, c), 1)
    rows(-1, 3, lambda row: put(e2, row + 1, post(r2, x2, uf2, us2, m2, i2, 2, 4, row)))
    rows(0, 2, lambda c: add(x1, 2, x1_in, 2, e2, c), 1)
    for at, row, coarse in ((0, -2, -1), (1, 5, 2)):
        outer = smooth(row_of(r_edge, at), m1_edge, i1_edge, at)
        inner = row_of(x1_in, (-1 if at == 0 else 4) + 2)
        for a in LEVELS:
            x1[row + 2, a] = outer[a] + e2[coarse + 1, a]
            x1[(-1 if at == 0 else 4) + 2, a] = inner[a] + e2[coarse + 1, a]
    rows(-1, 5, lambda row: put(e1, row + 1, post(r1_in, x1, uf1, us1, m1, i1, 2, 2, row)))
    rows(-1, 5, lambda c: add(x0, 2, x0_in, 3, e1, c), 1)
    rows(-1, 9, lambda row: put(z0, row + 1, post(r0, x0, uf0, us0, m0, i0, 3, 1, row)))

    def image(row):
        flux = None
        last = z0[row + 1, BLK - 1][:, :LANES]
        first_z = z0[row + 1, 0][:, :LANES]
        over = own[row, 3 * BLK + BLK - 1] * (up(first_z) - last)
        below = down(over)
        for a in LEVELS:
            wide = z0[row + 1, a]
            here = wide[:, :LANES]
            side = us0[row + 3, a] * (wide - turn(wide, -1))
            total = own[row, 5 * BLK + a] * here + (side - turn(side, 1))[:, :LANES]
            total = total + uf0[row + 3, a][:, :LANES] * (here - z0[row + 2, a][:, :LANES])
            total = total + uf0[row + 2, a][:, :LANES] * (here - z0[row, a][:, :LANES])
            if a < BLK - 1:
                flux = own[row, 3 * BLK + a] * (z0[row + 1, a + 1][:, :LANES] - here)
            else:
                flux = over
            total = total - flux + below
            below = flux
            w_own[row, a] = total
            z_own[row, a] = here
            if number < 2:
                r_next[row, a] = r_own[row, a] - THETA * total
        if number < 2:
            for g in range(BLK // PACK):
                values = [r_next[row, g * PACK + f] for f in range(PACK)]
                to_right[row, g] = packed(values, True)
                to_left[row, g] = packed(values, False)

    rows(0, OWN, image, 1)

    if number == 2:
        g_r0, g_z0, g_w0, g_z1, g_w1 = past

        def dots(row, acc):
            acc = list(acc)
            for a in LEVELS:
                z = (g_z0[row, a], g_z1[row, a], z_own[row, a])
                w = (g_w0[row, a], g_w1[row, a], w_own[row, a])
                r = (g_r0[row, a], first_r[row, a], r_own[row, a])
                terms = [r[i] * z[j] for i in range(3) for j in range(i + 1)]
                terms += [w[i] * z[j] for i in range(3) for j in range(3)]
                acc = [s + t for s, t in zip(acc, terms)]
            return tuple(acc)

        acc = lax.fori_loop(0, OWN, dots, tuple(jnp.zeros((SUB, LANES), F32) for _ in range(15)))
        gram[...] = jnp.zeros_like(gram)
        for i in range(15):
            gram[i : i + 1, :] = jnp.sum(acc[i], axis=0, keepdims=True)


def last_kernel(gram, r2, z0, z1, z2, w0, w1, w2, sol, res):
    get = lambda i: jnp.broadcast_to(jnp.sum(gram[i : i + 1, :], axis=1, keepdims=True), (SUB, LANES))
    q, at = {}, 0
    for i in range(3):
        for j in range(i + 1):
            q["r", i, j] = get(at)
            at += 1
    for i in range(3):
        for j in range(3):
            q["w", i, j] = get(at)
            at += 1
    zero = jnp.zeros((SUB, LANES), F32)

    def product(base, c, z):
        total = zero
        for j in range(3):
            if z[j] is None:
                continue
            term = q["r", base, j] if base is not None else zero
            for i in range(3):
                if c[i] is not None:
                    term = term + c[i] * q["w", i, j]
            total = total + z[j] * term
        return total

    one = zero + 1.0
    c = [None] * 3
    p = [one, None, None]
    gamma = q["r", 0, 0]
    x = [zero] * 3
    plus = lambda s, t: t if s is None else s + t
    for step in range(3):
        alpha = gamma / product(None, p, p)
        for j in range(step + 1):
            x[j] = x[j] + alpha * p[j]
            c[j] = plus(c[j], -(alpha * p[j]))
        if step == 2:
            break
        c[step] = c[step] + THETA
        z = [None] * 3
        z[step + 1] = one
        for i in range(step + 1):
            part = c[i] * (1.0 / THETA)
            z[i] = plus(z[i], part)
            z[i + 1] = plus(z[i + 1], -part)
        fresh = product(step + 1, c, z)
        beta = fresh / gamma
        p = [plus(z[j], beta * p[j]) if p[j] is not None else z[j] for j in range(3)]
        gamma = fresh

    def per_row(row, carry):
        for a in LEVELS:
            s = x[0] * z0[row, a] + x[1] * z1[row, a] + x[2] * z2[row, a]
            t = r2[row, a] + c[0] * w0[row, a] + c[1] * w1[row, a] + c[2] * w2[row, a]
            sol[pl.ds(a * OWN + row, NBLK, stride=BLK * OWN), :] = s[:NBLK]
            res[pl.ds(a * OWN + row, NBLK, stride=BLK * OWN), :] = t[:NBLK]
        return carry

    lax.fori_loop(0, OWN, per_row, 0)


def per_device(cotangent, courant, faces_first, faces_second, faces_vertical, damping, *blocks):
    n_rows = lax.axis_size(ROWS_AX)
    n_cols = lax.axis_size(COLS_AX)
    pos = jnp.stack([lax.axis_index(COLS_AX), lax.axis_index("tx") & 1]).astype(jnp.int32)
    pos, cotangent = lax.optimization_barrier((pos, cotangent))

    def send(x, dr, dc):
        route = [
            (r * n_cols + c, ((r + dr) % n_rows) * n_cols + (c + dc) % n_cols)
            for r in range(n_rows)
            for c in range(n_cols)
        ]
        return lax.ppermute(x, ALL, route)

    mates = [(r * n_cols + c, (r ^ 1) * n_cols + c) for r in range(n_rows) for c in range(n_cols)]

    def total_over(x, axis):
        size, done = lax.axis_size(axis), 1
        while done < size:
            count = 4 if size // done >= 4 else 2
            route = lambda by: [(i, (i + by) % size) for i in range(size)]
            shifts = (1, 2, -1)[: count - 1] if count == 4 else (1,)
            x = functools.reduce(jnp.add, [lax.ppermute(x, axis, route(k * done)) for k in shifts], x)
            done *= count
        return x

    flat = lambda x: x.reshape(x.shape[0] * OWN, LANES)
    wide = lambda n: shape(n, BLK, SUB, WIDE)
    tile = lambda *n: shape(*n, SUB, LANES)
    vwide = lambda n: pltpu.VMEM((n, BLK, SUB, WIDE), F32)

    own, msg_a, msg_b, to_right, to_left, start = pl.pallas_call(
        first_kernel,
        out_shape=[
            tile(OWN, 6 * BLK), tile(DEEP, 5 * BLK), tile(DEEP, 5 * BLK),
            tile(OWN, BLK), tile(OWN, BLK), tile(OWN, BLK),
        ],
        in_specs=[pl.BlockSpec(memory_space=pltpu.HBM)] * 6,
        out_specs=[VM] * 6,
        scratch_shapes=[pltpu.VMEM(((LEV - (i == 4)) * OWN, LANES), F32) for i in range(6)]
        + [pltpu.SemaphoreType.DMA((6,))],
        compiler_params=params(),
    )(*[pltpu.with_memory_space_constraint(flat(x), pltpu.HBM) for x in (cotangent, courant, faces_first, faces_second, faces_vertical, damping)])
    own_a, own_b = send(msg_a, 1, 0), send(msg_b, -1, 0)
    got_l, got_r = send(to_right, 0, 1), send(to_left, 0, -1)
    got_a = send(jnp.concatenate([got_l[-DEEP:], got_r[-DEEP:]], axis=1), 1, 0)
    got_b = send(jnp.concatenate([got_l[:DEEP], got_r[:DEEP]], axis=1), -1, 0)

    inner = call(
        functools.partial(inner_kernel, n_cols),
        [wide(8)] * 8 + [wide(4)] * 6,
        [pos, own, got_l, got_r],
    )
    x_own, inner = inner[1], [inner[0], *inner[2:]]
    outs = call(
        functools.partial(setup_kernel, n_cols),
        [wide(14)] * 5 + [wide(8)] * 4 + [wide(3)] * 4 + [tile(80)] * 2 + [tile(20)],
        [pos, own_a, own_b, got_a, got_b, *inner],
        [vwide(n) for n in (14, 14, 8, 8, 3, 3, 3, 3, 3, 3, 3, 3)],
    )
    r0, uf0, us0, m0, i0, uf1, us1, m1, i1, uf2, us2, m2, i2, up_co, down_co, far_co = outs
    c0, c1 = (uf0, us0, m0, i0), (uf1, us1, m1, i1)
    co_a, co_b = send(up_co, 1, 0), send(down_co, -1, 0)
    far_a, far_b = send(far_co, 2, 0), send(far_co, -2, 0)
    x0, r1, x1, r2, up_msg, down_msg = call(
        outset_kernel,
        [wide(14), wide(8), wide(8), wide(2), tile(20), tile(20)],
        [r0, x_own, *c0, *c1],
    )
    residuals, zs, ws = [start], [], []
    upward = [vwide(n) for n in (6, 5, 5, 3, 4, 6, 10, 8, 12, 2)] + [pltpu.VMEM((BLK, SUB, LANES), F32)]
    for number in range(3):
        if number:
            got_l, got_r = send(to_right, 0, 1), send(to_left, 0, -1)
            whole = jnp.concatenate([residuals[-1], got_l, got_r], axis=1)
            all_a, all_b = send(whole[OWN - DEEP :], 1, 0), send(whole[:DEEP], -1, 0)
            r0, x0, r1, x1, r2, up_msg, down_msg = call(
                functools.partial(again_kernel, n_cols),
                [wide(14)] * 2 + [wide(8)] * 2 + [wide(2)] + [tile(20)] * 2,
                [pos, residuals[-1], got_l, got_r, all_a, all_b, *c0, *c1],
            )
        msg_a, msg_b = send(up_msg, 1, 0), send(down_msg, -1, 0)
        if number == 0:
            coarse = call(
                coarse_kernel,
                [wide(2)] * 2 + [wide(6)] * 4 + [wide(5)] * 4,
                [uf2, us2, m2, i2, co_a, co_b, far_co, far_a, far_b],
            )
            edge1, c2, c3 = coarse[:2], coarse[2:6], coarse[6:]
        r2, x2, r3, msg = call(
            middle_kernel,
            [wide(6)] * 2 + [wide(1), tile(5)],
            [r2, msg_a, msg_b, *c2],
        )
        mate = lax.ppermute(msg, ALL, mates)
        both = call(join_kernel, [tile(BLK)], [msg, mate])[0]
        before, after = send(both, 2, 0), send(both, -2, 0)
        ins = [pos, residuals[-1], own, msg_a, msg_b, r3, mate, before, after, r0, x0, r1, x1, r2, x2]
        ins += [*c0, *c1, *edge1, *c2, *c3]
        if number == 2:
            ins += [residuals[0], zs[0], ws[0], zs[1], ws[1], residuals[1]]
        outs = [tile(OWN, BLK)] * 2
        outs += [tile(OWN, BLK), tile(OWN, 2), tile(OWN, 2)] if number < 2 else [shape(16, LANES)]
        outs = call(functools.partial(ascend_kernel, number), outs, ins, upward)
        zs.append(outs[0])
        ws.append(outs[1])
        if number < 2:
            residuals.append(outs[2])
            to_right, to_left = outs[3:]
        else:
            gram = outs[2]
    for axis in (COLS_AX, "tx", "panel"):
        gram = total_over(gram, axis)
    sol, res = call(
        last_kernel,
        [shape(LEV * OWN, LANES)] * 2,
        [gram, residuals[2], *zs, *ws],
    )
    return sol.reshape(LEV, OWN, LANES), res.reshape(LEV, OWN, LANES)


def solution(mesh):
    field = P(None, ROWS_AX, COLS_AX)
    block = P(None, None, None, ROWS_AX, COLS_AX)
    return jax.shard_map(
        per_device,
        mesh=mesh,
        in_specs=(field,) * 6 + (block,) * 4,
        out_specs=(field, field),
        check_vma=False,
    )
```
